32 devices in a mesh: groups: 2 (over y), band: 4 (over z), sub: 2 (over x), cfg: 2 (over core).
Axes of the slice: x: 2, y: 2, z: 4, core: 2. Of those that a mesh axis runs over, the one named last changes fastest.
Arguments:
- latents: float32 [32, 32, 256], P('groups', 'band', 'sub'), parts along dimension 0, may hold values from -6 to 6
- in_weight: bfloat16 [3, 3, 16, 320], replicated, may hold values from -0.5 to 0.5
- mid_weight: bfloat16 [3, 3, 320, 320], replicated, may hold values from -0.109375 to 0.109375
- out_weight: bfloat16 [3, 3, 16, 320], replicated, may hold values from -0.109375 to 0.109375
- norm_mean: float32 [2, 320], replicated, may hold values from -3 to 3
- norm_rstd: float32 [2, 320], replicated, may hold values from 0.5 to 2
- cond_embed: float32 [2, 640], P('cfg', 'groups'), parts along dimension 1, may hold values from -6 to 6
- time_embed: float32 [1000, 320], replicated, may hold values from -6 to 6
- time_index: int32 [2], replicated, may hold values from 0 to 999
- coef_index: int32 [2], replicated, may hold values from 0 to 999
- sampler_table: float32 [3, 1000], replicated, may hold values from -0.4 to 4, as said below
Outputs:
- denoised: float32 [32, 32, 256], P('groups', 'band', 'sub'), parts along dimension 0
The draws below stay inside these ranges and needn't reach their ends.
There are 2 independent parts, one for each index of `groups`. The reference program is written for one: setup_inputs(seed, part) draws one part's arguments, and reference() takes and returns one part's arrays. A program takes and returns all parts, laid end to end along the dimension named above; an argument that names none is the same for every part. Nothing has to cross between parts.
Inputs may be any that keep to these rules, and one draw needn't show every extreme that they name: `sampler_table`: column k holds one sampler step: row 0 scales the latent (0.8 to 1.2), row 1 scales the guided noise (-0.4 to -0.1), row 2 is the guidance scale (1.5 to 4.0).
All inputs are finite; a program needn't handle non-finite values.
Results may differ from the reference program's by a relative error of at most 0.013.
Values may be sent and summed in bfloat16 or wider, within the bound.
No kernel may reach another device: no remote copies, remote signals or barrier semaphores. Data moves between devices by JAX's collectives and lax.ppermute only.
A program may use at most 64 MiB of HBM per device.

```python
import math
import jax
import jax.numpy as jnp
from jax import lax

CH = 16
FEAT = 320
TSTEPS = 1000
NCOEF = 1000
STEPS = 2
ROWS_DEV = 8
HEIGHT = 32
WIDTH = 256


def draw_sampler_table(key, part):
    spread = jax.random.uniform(key, (3, NCOEF), jnp.float32)
    low_end = jnp.array([[0.8], [-0.4], [1.5]], jnp.float32)
    high_end = jnp.array([[1.2], [-0.1], [4.0]], jnp.float32)
    return low_end + (high_end - low_end) * spread


def steps_of(key, shape, cuts, smallest, high):
    def one(dim, blocks):
        draws = jax.random.uniform(jax.random.fold_in(jax.random.fold_in(key, 6), dim), (blocks,), jnp.float32, smallest / len(cuts), high / len(cuts))
        return jnp.repeat(jnp.exp(draws), shape[dim] // blocks).reshape((-1,) + (1,) * (len(shape) - dim - 1))

    factor_of = one(*cuts[0])
    for cut in cuts[1:]:
        factor_of = factor_of * one(*cut)
    return factor_of


def scatter_about(key, shape, deviation, reach, split=(), held_as=jnp.bfloat16):
    entries = jax.random.normal(key, shape, jnp.float32) * deviation
    if len(split) > 0:
        entries = steps_of(key, shape, split, -0.22, 0.18) * entries
    return jnp.clip(entries, min=-reach, max=reach).astype(held_as)


def setup_inputs(seed: int = 0, part: int = 0) -> dict:
    key_of = jax.random.split(jax.random.key(seed), 12)
    part_keys = jax.random.split(jax.random.fold_in(key_of[11], part), 12)
    latents = scatter_about(part_keys[0], (CH, HEIGHT, WIDTH), 1.0, 6.0, ((1, 4), (2, 2)), jnp.float32)
    in_weight = scatter_about(key_of[1], (3, 3, CH, FEAT), (9 * CH) ** -0.5, 0.5)
    mid_weight = scatter_about(key_of[2], (3, 3, FEAT, FEAT), (9 * FEAT) ** -0.5, 0.109375)
    out_weight = scatter_about(key_of[3], (3, 3, CH, FEAT), (9 * FEAT) ** -0.5, 0.109375)
    norm_mean = scatter_about(key_of[4], (2, FEAT), 0.5, 3.0, (), jnp.float32)
    norm_rstd = jnp.clip(jnp.exp(jax.random.uniform(key_of[5], (2, FEAT), jnp.float32, math.log(0.5), math.log(2.0))), 0.5, 2.0)
    cond_embed = scatter_about(part_keys[6], (2, FEAT), 1.0, 6.0, ((0, 2),), jnp.float32)
    time_embed = scatter_about(key_of[7], (TSTEPS, FEAT), 1.0, 6.0, (), jnp.float32)
    time_index = jax.random.randint(key_of[8], (STEPS,), 0, TSTEPS).astype(jnp.int32)
    coef_index = jax.random.randint(key_of[9], (STEPS,), 0, NCOEF).astype(jnp.int32)
    sampler_table = draw_sampler_table(jax.random.fold_in(key_of[11], 71), part)
    return dict(latents=latents, in_weight=in_weight, mid_weight=mid_weight, out_weight=out_weight, norm_mean=norm_mean, norm_rstd=norm_rstd, cond_embed=cond_embed, time_embed=time_embed, time_index=time_index, coef_index=coef_index, sampler_table=sampler_table)


def conv_valid(source, kernel, pattern):
    out_rows = source.shape[1] - 2
    out_cols = source.shape[2] - 2
    total = None
    for tap_row in range(3):
        for tap_col in range(3):
            window = source[:, tap_row:tap_row + out_rows, tap_col:tap_col + out_cols].astype(jnp.float32)
            product = jnp.einsum(pattern, kernel[tap_row, tap_col].astype(jnp.float32), window, precision=lax.Precision.HIGHEST)
            total = product if total is None else total + product
    return total


def activate(field, centre, spread):
    return jax.nn.silu((field - centre[:, None, None]) * spread[:, None, None]).astype(jnp.bfloat16)


def noise_region(source, inside, kernels, offset):
    in_weight, mid_weight, out_weight, norm_mean, norm_rstd = kernels
    first_map = conv_valid(source * inside, in_weight, "co,chw->ohw") + offset[:, None, None]
    lifted = activate(first_map, norm_mean[0], norm_rstd[0]) * inside[1:-1, 1:-1]
    second = first_map[:, 1:-1, 1:-1] + conv_valid(lifted, mid_weight, "oc,chw->ohw")
    lowered = activate(second, norm_mean[1], norm_rstd[1]) * inside[2:-2, 2:-2]
    return conv_valid(lowered, out_weight, "oc,chw->ohw")


def noise_field(source, offset, kernels):
    height = source.shape[1]
    width = source.shape[2]
    padded = jnp.pad(source, ((0, 0), (3, 3), (3, 3)))
    row_place = jnp.arange(height + 6, dtype=jnp.int32) - 3
    col_place = jnp.arange(width + 6, dtype=jnp.int32) - 3
    col_inside = (col_place >= 0) & (col_place < width)
    block_count = height // ROWS_DEV

    def one_block(block_id):
        start = (block_id * ROWS_DEV).astype(jnp.int32)
        piece = lax.dynamic_slice_in_dim(padded, start, ROWS_DEV + 6, 1)
        rows_here = lax.dynamic_slice_in_dim(row_place, start, ROWS_DEV + 6, 0)
        row_inside = (rows_here >= 0) & (rows_here < height)
        inside = (row_inside[:, None] & col_inside[None, :]).astype(jnp.bfloat16)
        return noise_region(piece, inside, kernels, offset)

    pieces = lax.map(one_block, jnp.arange(block_count, dtype=jnp.int32))
    return jnp.transpose(pieces, (1, 0, 2, 3)).reshape(source.shape[0], height, width)


def reference(latents, in_weight, mid_weight, out_weight, norm_mean, norm_rstd, cond_embed, time_embed, time_index, coef_index, sampler_table):
    kernels = (in_weight, mid_weight, out_weight, norm_mean, norm_rstd)
    current = latents
    for sample_step in range(STEPS):
        time_row = lax.dynamic_index_in_dim(time_embed, time_index[sample_step], 0, keepdims=False)
        sampler_col = lax.dynamic_index_in_dim(sampler_table, coef_index[sample_step], 1, keepdims=False)
        source = current.astype(jnp.bfloat16)
        plain_noise = noise_field(source, time_row + cond_embed[0], kernels)
        steered_noise = noise_field(source, time_row + cond_embed[1], kernels)
        guided = plain_noise + sampler_col[2] * (steered_noise - plain_noise)
        current = sampler_col[0] * current + sampler_col[1] * guided
    return current
```

```python
import jax
import jax.numpy as jnp
import numpy as np
from jax import lax
from jax.experimental import pallas as pl
from jax.experimental.pallas import tpu as pltpu
from jax.sharding import PartitionSpec as P

TILE = 256
BF = jnp.bfloat16
F32 = jnp.float32


def ceil_to(value, unit):
    return -(-value // unit) * unit


class Plan:
    def __init__(self, rows, half, steps, chans, feat):
        self.rows, self.half, self.steps = rows, half, steps
        self.chans, self.feat = chans, feat
        self.margin = 3 * steps
        self.stride = half + 2 * self.margin
        self.src_rows = [rows + 2 * (self.margin - 3 * s) for s in range(steps)]
        self.lift_tiles = [-(-(r - 2) * self.stride // TILE) for r in self.src_rows]
        self.mid_tiles = [-(-(r - 4) * self.stride // TILE) for r in self.src_rows]
        self.lift_width = max(self.lift_tiles) * TILE
        self.width = ceil_to(self.lift_width + 3 * self.stride + 3, 128)
        self.depth = ceil_to(9 * (feat + chans), 128)


def act(pre, scale, shift):
    u = pre * scale + shift
    return u + u * jnp.tanh(u)


def body(plan, cfg_ref, coef_ref, own_ref, up_ref, dn_ref, side_ref, wbig_ref, win_ref, wout_ref, aff_ref,
         mask_ref, out_ref, row_ref, state_ref, src_ref, lift_ref, z_ref):
    stride, chans, feat, steps = plan.stride, plan.chans, plan.feat, plan.steps
    rows, margin, half = plan.rows, plan.margin, plan.half
    first = cfg_ref[0] == 0
    span = own_ref.shape[1]

    for y in range(rows + 2 * margin):
        if y < margin:
            row = up_ref[y].astype(F32)
        elif y < margin + rows:
            row = own_ref[pl.ds(y - margin, chans, stride=rows), :]
        else:
            row = dn_ref[y - margin - rows].astype(F32)
        side = side_ref[y].astype(F32)
        low = jnp.concatenate([side, row[:, : half + margin]], axis=1)
        high = jnp.concatenate([row[:, span - half - margin :], side], axis=1)
        state_ref[:, y * stride : (y + 1) * stride] = jnp.where(first, low, high)

    for s in range(steps):
        n_src = plan.src_rows[s]
        lt, mt = plan.lift_tiles[s], plan.mid_tiles[s]
        filled = n_src * stride
        if s == 0:
            src_ref[:, :filled] = state_ref[:, :filled].astype(BF)
        else:
            src_ref[:, :filled] = (
                state_ref[:, :filled] * mask_ref[3 * s + 2 : 3 * s + 3, :filled]
            ).astype(BF)
        col = 2 + 4 * s

        def shifted(ref, base, extra):
            return [
                ref[:, base + (i + extra) * stride + j + extra : base + (i + extra) * stride + j + extra + TILE]
                for i in range(3)
                for j in range(3)
            ]

        for t in range(lt):
            base = t * TILE
            window = jnp.concatenate(shifted(src_ref, base, 0), axis=0)
            pre = jnp.dot(win_ref[...], window, preferred_element_type=F32)
            keep = mask_ref[3 * s : 3 * s + 1, base : base + TILE]
            for q in range(2):
                val = act(pre, aff_ref[:, 0:1], aff_ref[:, col + q : col + q + 1])
                lift_ref[q, :, base : base + TILE] = (val * keep).astype(BF)
        for q in range(2):
            for t in range(mt):
                base = t * TILE
                taps = shifted(lift_ref.at[q], base, 0) + shifted(src_ref, base, 1)
                rest = plan.depth - 9 * (feat + chans)
                if rest:
                    taps = taps + [jnp.zeros((rest, TILE), BF)]
                pre = jnp.dot(wbig_ref[...], jnp.concatenate(taps, axis=0), preferred_element_type=F32)
                keep = mask_ref[3 * s + 1 : 3 * s + 2, base : base + TILE]
                val = act(pre, aff_ref[:, 1:2], aff_ref[:, col + 2 + q : col + 3 + q])
                low = (val * keep).astype(BF)
                z_ref[q, :, base : base + TILE] = jnp.dot(wout_ref[...], low, preferred_element_type=F32)
        ca, cb, cg = coef_ref[s, 0], coef_ref[s, 1], coef_ref[s, 2]
        done = (n_src - 6) * stride
        total = None
        for k in range(9):
            off = (k // 3) * stride + k % 3
            block = slice(k * chans, (k + 1) * chans)
            plain = z_ref[0, block, off : off + done]
            steered = z_ref[1, block, off : off + done]
            piece = plain + cg * (steered - plain)
            total = piece if total is None else total + piece
        kept = state_ref[:, 3 * stride + 3 : 3 * stride + 3 + done]
        state_ref[:, :done] = ca * kept + cb * total

    for y in range(rows):
        out_ref[pl.ds(y, chans, stride=rows), :] = state_ref[:, y * stride : y * stride + half]


def ring(axis, step):
    count = lax.axis_size(axis)
    return [(i, i + step) for i in range(count) if 0 <= i + step < count]


def shards(latents, in_weight, mid_weight, out_weight, norm_mean, norm_rstd, cond_embed, time_embed,
           time_index, coef_index, sampler_table):
    chans, rows, cols = latents.shape
    feat = mid_weight.shape[2]
    steps = time_index.shape[0]
    half = cols // 2
    plan = Plan(rows, half, steps, chans, feat)
    margin, stride = plan.margin, plan.stride
    side_rows = rows + 2 * margin

    cfg = lax.axis_index("cfg")
    subs = lax.axis_size("sub")
    lat_t = jnp.transpose(latents, (1, 0, 2)).astype(BF)
    up = lax.ppermute(lat_t[rows - margin :], "band", ring("band", 1))
    dn = lax.ppermute(lat_t[:margin], "band", ring("band", -1))
    other_cond = lax.ppermute(cond_embed, "cfg", [(0, 1), (1, 0)])
    full = jnp.concatenate([up, lat_t, dn], axis=0)
    strip = jnp.where(cfg == 1, full[:, :, cols - margin :], full[:, :, :margin])
    pairs = []
    for i in range(subs - 1):
        pairs += [(2 * i + 1, 2 * i + 2), (2 * i + 2, 2 * i + 1)]
    side = lax.ppermute(strip, ("sub", "cfg"), pairs)

    conds = jnp.where(cfg == 0, jnp.concatenate([cond_embed, other_cond]), jnp.concatenate([other_cond, cond_embed]))
    times = jnp.take(time_embed, time_index, axis=0)
    halved = 0.5 * norm_rstd
    columns = [halved[0], halved[1]]
    for s in range(steps):
        for k in range(2):
            for q in range(2):
                columns.append((times[s] + conds[q] - norm_mean[k]) * halved[k])
    aff = jnp.stack(columns, axis=1)
    coef = jnp.take(sampler_table, coef_index, axis=1).T

    flat = np.arange(plan.width)
    ys, xs = flat // stride, flat % stride
    top = lax.axis_index("band") * rows
    left = lax.axis_index("sub") * cols + cfg * half
    height = rows * lax.axis_size("band")
    breadth = cols * subs
    masks = []
    for m in range(margin - 1, -1, -1):
        gy = top - m + jnp.asarray(ys, jnp.int32)
        gx = left - m + jnp.asarray(xs, jnp.int32)
        masks.append((gy >= 0) & (gy < height) & (gx >= 0) & (gx < breadth))
    mask = jnp.stack(masks).astype(F32)
    order = []
    for s in range(steps):
        order += [mask[3 * s], mask[3 * s + 1], mask[3 * s - 1] if s else mask[0]]
    mask = jnp.stack(order)

    wmid = jnp.transpose(mid_weight, (2, 0, 1, 3)).reshape(feat, 9 * feat)
    win = jnp.transpose(in_weight, (3, 0, 1, 2)).reshape(feat, 9 * chans)
    wbig = jnp.concatenate([wmid, win, jnp.zeros((feat, plan.depth - 9 * (feat + chans)), BF)], axis=1)
    wout = out_weight.reshape(9 * chans, feat)

    vmem = pl.BlockSpec(memory_space=pltpu.VMEM)
    smem = pl.BlockSpec(memory_space=pltpu.SMEM)
    mine = pl.pallas_call(
        lambda *refs: body(plan, *refs),
        out_shape=jax.ShapeDtypeStruct((chans * rows, half), F32),
        in_specs=[smem, smem] + [vmem] * 9,
        out_specs=vmem,
        scratch_shapes=[
            pltpu.VMEM((chans, 384), F32),
            pltpu.VMEM((chans, plan.width), F32),
            pltpu.VMEM((chans, plan.width), BF),
            pltpu.VMEM((2, feat, plan.lift_width), BF),
            pltpu.VMEM((2, 9 * chans, plan.lift_width), F32),
        ],
        compiler_params=pltpu.CompilerParams(vmem_limit_bytes=48 * 1024 * 1024),
        name="denoise",
    )(cfg.reshape(1), coef, latents.reshape(chans * rows, cols), up, dn, side, wbig, win, wout, aff, mask)
    theirs = lax.ppermute(mine, "cfg", [(0, 1), (1, 0)])
    whole = jnp.where(
        cfg == 0, jnp.concatenate([mine, theirs], axis=1), jnp.concatenate([theirs, mine], axis=1)
    )
    return whole.reshape(chans, rows, cols)


def solution(mesh):
    return jax.shard_map(
        shards,
        mesh=mesh,
        in_specs=(P("groups", "band", "sub"), P(), P(), P(), P(), P(), P("cfg", "groups"), P(), P(), P(), P()),
        out_specs=P("groups", "band", "sub"),
        check_vma=False,
    )
```

```python
import jax
import jax.numpy as jnp
from jax import lax
from jax.experimental import pallas as pl
from jax.experimental.pallas import tpu as pltpu
from jax.sharding import PartitionSpec as P

TILE = 256
BF = jnp.bfloat16
F32 = jnp.float32
VMEM = pl.BlockSpec(memory_space=pltpu.VMEM)
SMEM = pl.BlockSpec(memory_space=pltpu.SMEM)
HBM = pl.BlockSpec(memory_space=pl.ANY)
PARAMS = pltpu.CompilerParams(vmem_limit_bytes=48 * 1024 * 1024)


def ceil_to(value, unit):
    return -(-value // unit) * unit


class Plan:
    def __init__(self, rows, half, steps, chans, feat):
        self.rows, self.half, self.steps = rows, half, steps
        self.chans, self.feat = chans, feat
        self.margin = 3 * steps
        self.span = rows + 2 * self.margin
        self.stride = half + 2 * self.margin
        self.src_rows = [self.span - 6 * s for s in range(steps)]
        self.lift = [ceil_to((r - 2) // 2 * self.stride, TILE) for r in self.src_rows]
        self.mid = [ceil_to((r - 4) // 2 * self.stride, 128) for r in self.src_rows]
        self.lift = [
            max(a, ceil_to(b + self.stride + 2, TILE)) for a, b in zip(self.lift, self.mid)
        ]
        self.block = ceil_to(max(self.lift) + 3 * self.stride + 4, 128)
        self.taps = 9 * feat
        self.depth = ceil_to(9 * (feat + chans), 128)
        self.levels = 3 * steps


def act(pre, scale, shift):
    u = pre * scale + shift
    return u + u * jnp.tanh(u)


def prep_body(plan, names, time_ref, table_ref, own_ref, other_ref, mean_ref, rstd_ref, mid_ref, in_ref,
              wbig_ref, win_ref, aff_ref, mask_ref, times_ref, rows_ref, sem):
    feat, chans, steps, stride = plan.feat, plan.chans, plan.steps, plan.stride
    band, sub, cfg = names
    copies = [
        pltpu.make_async_copy(table_ref.at[pl.ds(time_ref[s], 1)], times_ref.at[pl.ds(s, 1)], sem.at[s])
        for s in range(steps)
    ]
    for copy in copies:
        copy.start()
    for k in range(9):
        wbig_ref[:, k * feat : (k + 1) * feat] = mid_ref[k * feat : (k + 1) * feat, :]
    turned = jnp.transpose(in_ref[...].astype(F32)).astype(BF)
    win_ref[...] = turned
    wbig_ref[:, plan.taps : plan.taps + 9 * chans] = turned
    rest = plan.depth - 9 * (feat + chans)
    if rest:
        wbig_ref[:, plan.depth - rest :] = jnp.zeros((feat, rest), BF)

    plain = lax.axis_index(cfg) == 0
    conds = [
        jnp.where(plain, own_ref[...], other_ref[...]),
        jnp.where(plain, other_ref[...], own_ref[...]),
    ]
    for copy in copies:
        copy.wait()
    rows_ref[...] = jnp.zeros(rows_ref.shape, F32)
    halved = 0.5 * rstd_ref[...]
    rows_ref[0:2, :feat] = halved
    for s in range(steps):
        for k in range(2):
            for q in range(2):
                line = 2 + 4 * s + 2 * k + q
                offset = times_ref[s : s + 1, :] + conds[q] - mean_ref[k : k + 1, :]
                rows_ref[line : line + 1, :feat] = offset * halved[k : k + 1, :]
    aff_ref[...] = jnp.transpose(rows_ref[...])[:feat, :]

    flat = lax.broadcasted_iota(jnp.int32, (8, plan.block), 1)
    ys = jnp.floor((flat.astype(F32) + 0.5) * (1.0 / stride)).astype(jnp.int32)
    xs = flat - ys * stride
    top = lax.axis_index(band) * plan.rows
    left = (lax.axis_index(sub) * 2 + lax.axis_index(cfg)) * plan.half
    height = plan.rows * lax.axis_size(band)
    breadth = 2 * plan.half * lax.axis_size(sub)
    for level in range(plan.levels):
        edge = plan.margin - 1 - level
        gx = xs + (left - edge)
        inx = (gx >= 0) & (gx < breadth)
        for b in range(2):
            gy = 2 * ys + (top - edge + b)
            keep = inx & (gy >= 0) & (gy < height)
            line = 2 * level + b
            mask_ref[line : line + 1, :] = jnp.where(keep, 1.0, 0.0)[0:1, :]


def field_row(plan, y, up_ref, own_ref, dn_ref, tail):
    if y < plan.margin:
        return up_ref[pl.ds(tail - plan.margin + y, plan.chans, stride=tail), :]
    if y < plan.margin + plan.rows:
        return own_ref[pl.ds(y - plan.margin, plan.chans, stride=plan.rows), :]
    return dn_ref[pl.ds(y - plan.margin - plan.rows, plan.chans, stride=tail), :]


def pack_body(plan, tail, cfg, up_ref, own_ref, dn_ref, out_ref):
    right = lax.axis_index(cfg) == 1
    width, margin = own_ref.shape[1], plan.margin
    for y in range(plan.span):
        row = field_row(plan, y, up_ref, own_ref, dn_ref, tail)
        out_ref[:, y * margin : (y + 1) * margin] = jnp.where(right, row[:, width - margin :], row[:, :margin])


def main_body(plan, tail, cfg, index_ref, table_ref, own_ref, up_ref, dn_ref, side_ref, wbig_ref, win_ref, wout_ref,
              aff_ref, mask_ref, out_ref, state_ref, src_ref, lift_ref, taps_ref, ext_ref, low_ref, z_ref):
    stride, chans, feat, steps = plan.stride, plan.chans, plan.feat, plan.steps
    margin, half = plan.margin, plan.half
    first = lax.axis_index(cfg) == 0
    width = own_ref.shape[1]

    for y in range(plan.span):
        row = field_row(plan, y, up_ref, own_ref, dn_ref, tail)
        side = side_ref[:, y * margin : (y + 1) * margin]
        low = jnp.concatenate([side, row[:, : half + margin]], axis=1)
        high = jnp.concatenate([row[:, width - half - margin :], side], axis=1)
        lane = y // 2 * stride
        state_ref[y % 2, :, lane : lane + stride] = jnp.where(first, low, high)
    ext_ref[9 * chans :, :] = jnp.zeros((ext_ref.shape[0] - 9 * chans, ext_ref.shape[1]), BF)

    def taken(ref, row, col, start, count):
        lane = row // 2 * stride + col + start
        return ref[row % 2, :, lane : lane + count]

    for s in range(steps):
        n_src = plan.src_rows[s]
        lift, mid = plan.lift[s], plan.mid[s]
        filled = n_src // 2 * stride
        for b in range(2):
            value = state_ref[b, :, :filled]
            if s:
                line = 2 * (3 * s - 1) + b
                value = value * mask_ref[line : line + 1, :filled]
            src_ref[b, :, :filled] = value.astype(BF)
        col = 2 + 4 * s
        for b in range(2):
            for k in range(9):
                i, j = k // 3, k % 3
                ext_ref[k * chans : (k + 1) * chans, b * mid : (b + 1) * mid] = taken(
                    src_ref, b + 1 + i, 1 + j, 0, mid
                )
        for b in range(2):
            line = 6 * s + b
            for base in range(0, lift, TILE):
                window = jnp.concatenate(
                    [taken(src_ref, b + k // 3, k % 3, base, TILE) for k in range(9)], axis=0
                )
                pre = jnp.dot(win_ref[...], window, preferred_element_type=F32)
                keep = mask_ref[line : line + 1, base : base + TILE]
                for q in range(2):
                    val = act(pre, aff_ref[:, 0:1], aff_ref[:, col + q : col + q + 1])
                    lift_ref[q, b, :, base : base + TILE] = (val * keep).astype(BF)
        for q in range(2):
            for bb in range(4):
                for j in range(3):
                    taps_ref[q, j, :, bb * mid : (bb + 1) * mid] = taken(lift_ref.at[q], bb, j, 0, mid)
        for q in range(2):
            for base in range(0, 2 * mid, TILE):
                window = [
                    taps_ref[q, k % 3, :, k // 3 * mid + base : k // 3 * mid + base + TILE] for k in range(9)
                ]
                window.append(ext_ref[:, base : base + TILE])
                pre = jnp.dot(wbig_ref[...], jnp.concatenate(window, axis=0), preferred_element_type=F32)
                val = act(pre, aff_ref[:, 1:2], aff_ref[:, col + 2 + q : col + 3 + q])
                for part in range(0, TILE, 128):
                    b, lane = (base + part) // mid, (base + part) % mid
                    line = 6 * s + 2 + b
                    keep = mask_ref[line : line + 1, lane : lane + 128]
                    low_ref[q, :, base + part : base + part + 128] = (val[:, part : part + 128] * keep).astype(BF)
        for q in range(2):
            z_ref[q, :, : 2 * mid] = jnp.dot(wout_ref[...], low_ref[q, :, : 2 * mid], preferred_element_type=F32)
        pick = index_ref[s]
        ca, cb, cg = table_ref[0, pick], table_ref[1, pick], table_ref[2, pick]
        done = (n_src - 6) // 2 * stride
        fresh = []
        for b in range(2):
            total = None
            for k in range(9):
                row = b + k // 3
                lane = row % 2 * mid + row // 2 * stride + k % 3
                block = slice(k * chans, (k + 1) * chans)
                plain = z_ref[0, block, lane : lane + done]
                steered = z_ref[1, block, lane : lane + done]
                piece = plain + cg * (steered - plain)
                total = piece if total is None else total + piece
            fresh.append(ca * taken(state_ref, b + 3, 3, 0, done) + cb * total)
        for b in range(2):
            state_ref[b, :, :done] = fresh[b]

    for y in range(plan.rows):
        lane = y // 2 * stride
        out_ref[pl.ds(y, chans, stride=plan.rows), :] = state_ref[y % 2, :, lane : lane + half]


def ring(axis, step):
    count = lax.axis_size(axis)
    return [(i, i + step) for i in range(count) if 0 <= i + step < count]


def shards(latents, in_weight, mid_weight, out_weight, norm_mean, norm_rstd, cond_embed, time_embed,
           time_index, coef_index, sampler_table):
    chans, rows, cols = latents.shape
    feat = mid_weight.shape[2]
    steps = time_index.shape[0]
    half = cols // 2
    plan = Plan(rows, half, steps, chans, feat)
    margin = plan.margin
    cfg = lax.axis_index("cfg")
    swap = [(0, 1), (1, 0)]

    tail = min(rows, ceil_to(margin, 8))
    other = lax.ppermute(cond_embed, "cfg", swap)
    up = lax.ppermute(latents[:, rows - tail :], "band", ring("band", 1)).reshape(chans * tail, cols)
    dn = lax.ppermute(latents[:, :tail], "band", ring("band", -1)).reshape(chans * tail, cols)
    own = latents.reshape(chans * rows, cols)

    wbig, win, aff, mask = pl.pallas_call(
        lambda *refs: prep_body(plan, ("band", "sub", "cfg"), *refs),
        out_shape=[
            jax.ShapeDtypeStruct((feat, plan.depth), BF),
            jax.ShapeDtypeStruct((feat, 9 * chans), BF),
            jax.ShapeDtypeStruct((feat, 128), F32),
            jax.ShapeDtypeStruct((2 * plan.levels, plan.block), F32),
        ],
        in_specs=[SMEM, HBM] + [VMEM] * 6,
        out_specs=[VMEM] * 4,
        scratch_shapes=[
            pltpu.VMEM((steps, feat), F32),
            pltpu.VMEM((128, ceil_to(feat, 128)), F32),
            pltpu.SemaphoreType.DMA((steps,)),
        ],
        compiler_params=PARAMS,
        name="prep",
    )(time_index, time_embed, cond_embed, other, norm_mean, norm_rstd,
      mid_weight.reshape(9 * feat, feat), in_weight.reshape(9 * chans, feat))

    strip = pl.pallas_call(
        lambda *refs: pack_body(plan, tail, "cfg", *refs),
        out_shape=jax.ShapeDtypeStruct((chans, ceil_to(plan.span * margin, 128)), F32),
        in_specs=[VMEM] * 3,
        out_specs=VMEM,
        name="pack",
    )(up, own, dn)
    subs = lax.axis_size("sub")
    pairs = []
    for i in range(subs - 1):
        pairs += [(2 * i + 1, 2 * i + 2), (2 * i + 2, 2 * i + 1)]
    side = lax.ppermute(strip, ("sub", "cfg"), pairs)

    lift, mid = max(plan.lift), max(plan.mid)
    mine = pl.pallas_call(
        lambda *refs: main_body(plan, tail, "cfg", *refs),
        out_shape=jax.ShapeDtypeStruct((chans * rows, half), F32),
        in_specs=[SMEM, SMEM] + [VMEM] * 9,
        out_specs=VMEM,
        scratch_shapes=[
            pltpu.VMEM((2, chans, plan.block), F32),
            pltpu.VMEM((2, chans, plan.block), BF),
            pltpu.VMEM((2, 2, feat, lift), BF),
            pltpu.VMEM((2, 3, feat, 4 * mid), BF),
            pltpu.VMEM((plan.depth - plan.taps, 2 * mid), BF),
            pltpu.VMEM((2, feat, 2 * mid), BF),
            pltpu.VMEM((2, 9 * chans, 2 * mid + 128), F32),
        ],
        compiler_params=PARAMS,
        name="denoise",
    )(coef_index, sampler_table, own, up, dn, side, wbig, win, out_weight.reshape(9 * chans, feat), aff, mask)
    theirs = lax.ppermute(mine, "cfg", swap)
    whole = jnp.where(
        cfg == 0, jnp.concatenate([mine, theirs], axis=1), jnp.concatenate([theirs, mine], axis=1)
    )
    return whole.reshape(chans, rows, cols)


def solution(mesh):
    return jax.shard_map(
        shards,
        mesh=mesh,
        in_specs=(P("groups", "band", "sub"), P(), P(), P(), P(), P(), P("cfg", "groups"), P(), P(), P(), P()),
        out_specs=P("groups", "band", "sub"),
        check_vma=False,
    )
```

```python
import jax
import jax.numpy as jnp
from jax import lax
from jax.experimental import pallas as pl
from jax.experimental.pallas import tpu as pltpu
from jax.sharding import PartitionSpec as P

TILE = 256
BF = jnp.bfloat16
F32 = jnp.float32
VMEM = pl.BlockSpec(memory_space=pltpu.VMEM)
SMEM = pl.BlockSpec(memory_space=pltpu.SMEM)
HBM = pl.BlockSpec(memory_space=pl.ANY)
PARAMS = pltpu.CompilerParams(vmem_limit_bytes=40 * 1024 * 1024)
SMALL = pltpu.CompilerParams(vmem_limit_bytes=8 * 1024 * 1024)


def ceil_to(value, unit):
    return -(-value // unit) * unit


class Plan:
    def __init__(self, rows, half, steps, chans, feat):
        self.rows, self.half, self.steps = rows, half, steps
        self.chans, self.feat = chans, feat
        self.margin = 3 * steps
        self.span = rows + 2 * self.margin
        self.stride = half + 2 * self.margin
        self.src_rows = [self.span - 6 * s for s in range(steps)]
        self.lift = [ceil_to((r - 2) // 2 * self.stride, TILE) for r in self.src_rows]
        self.mid = [ceil_to((r - 4) // 2 * self.stride, 128) for r in self.src_rows]
        self.lift = [
            max(a, ceil_to(b + self.stride + 2, TILE)) for a, b in zip(self.lift, self.mid)
        ]
        self.block = ceil_to(max(self.lift) + 3 * self.stride + 4, 128)
        self.taps = 9 * feat
        self.depth = ceil_to(9 * (feat + chans), 128)
        self.levels = 3 * steps


def act(pre, scale, shift):
    scale = jnp.concatenate([scale] * (pre.shape[1] // 128), axis=1)
    shift = jnp.concatenate([shift] * (pre.shape[1] // 128), axis=1)
    u = pre * scale + shift
    return u + u * jnp.tanh(u)


def prep_body(plan, names, times_ref, own_ref, other_ref, mean_ref, rstd_ref, mid_ref, in_ref,
              wbig_ref, win_ref, aff_ref, mask_ref, rows_ref):
    feat, chans, steps, stride = plan.feat, plan.chans, plan.steps, plan.stride
    band, sub, cfg = names
    for k in range(9):
        wbig_ref[:, k * feat : (k + 1) * feat] = mid_ref[k * feat : (k + 1) * feat, :]
    turned = jnp.transpose(in_ref[...].astype(F32)).astype(BF)
    win_ref[...] = turned
    wbig_ref[:, plan.taps : plan.taps + 9 * chans] = turned
    rest = plan.depth - 9 * (feat + chans)
    if rest:
        wbig_ref[:, plan.depth - rest :] = jnp.zeros((feat, rest), BF)

    plain = lax.axis_index(cfg) == 0
    conds = [
        jnp.where(plain, own_ref[...], other_ref[...]),
        jnp.where(plain, other_ref[...], own_ref[...]),
    ]
    rows_ref[...] = jnp.zeros(rows_ref.shape, F32)
    halved = 0.5 * rstd_ref[...]
    rows_ref[0:2, :feat] = halved
    for s in range(steps):
        for k in range(2):
            for q in range(2):
                line = 2 + 4 * s + 2 * k + q
                offset = times_ref[s : s + 1, :] + conds[q] - mean_ref[k : k + 1, :]
                rows_ref[line : line + 1, :feat] = offset * halved[k : k + 1, :]
    turned = jnp.transpose(rows_ref[...])[:feat, :]
    for line in range(2 + 4 * steps):
        aff_ref[line] = jnp.broadcast_to(turned[:, line : line + 1], (feat, 128))

    flat = lax.broadcasted_iota(jnp.int32, (8, plan.block), 1)
    ys = jnp.floor((flat.astype(F32) + 0.5) * (1.0 / stride)).astype(jnp.int32)
    xs = flat - ys * stride
    top = lax.axis_index(band) * plan.rows
    left = (lax.axis_index(sub) * 2 + lax.axis_index(cfg)) * plan.half
    height = plan.rows * lax.axis_size(band)
    breadth = 2 * plan.half * lax.axis_size(sub)
    for level in range(plan.levels):
        edge = plan.margin - 1 - level
        gx = xs + (left - edge)
        inx = (gx >= 0) & (gx < breadth)
        for b in range(2):
            gy = 2 * ys + (top - edge + b)
            keep = inx & (gy >= 0) & (gy < height)
            line = 2 * level + b
            mask_ref[line : line + 1, :] = jnp.where(keep, 1.0, 0.0)[0:1, :]


def field_row(plan, y, up_ref, own_ref, dn_ref, tail):
    if y < plan.margin:
        return up_ref[pl.ds(tail - plan.margin + y, plan.chans, stride=tail), :]
    if y < plan.margin + plan.rows:
        return own_ref[pl.ds(y - plan.margin, plan.chans, stride=plan.rows), :]
    return dn_ref[pl.ds(y - plan.margin - plan.rows, plan.chans, stride=tail), :]


def pack_body(plan, tail, cfg, up_ref, own_ref, dn_ref, after_ref, out_ref):
    del after_ref
    right = lax.axis_index(cfg) == 1
    width, margin = own_ref.shape[1], plan.margin
    for y in range(plan.span):
        row = field_row(plan, y, up_ref, own_ref, dn_ref, tail)
        out_ref[:, y * margin : (y + 1) * margin] = jnp.where(right, row[:, width - margin :], row[:, :margin])


def main_body(plan, tail, cfg, index_ref, table_ref, own_ref, up_ref, dn_ref, side_ref, wbig_ref, win_ref, wout_ref,
              aff_ref, mask_ref, out_ref, state_ref, src_ref, lift_ref, taps_ref, ext_ref, low_ref, z_ref):
    stride, chans, feat, steps = plan.stride, plan.chans, plan.feat, plan.steps
    margin, half = plan.margin, plan.half
    first = lax.axis_index(cfg) == 0
    width = own_ref.shape[1]

    for y in range(plan.span):
        row = field_row(plan, y, up_ref, own_ref, dn_ref, tail)
        side = side_ref[:, y * margin : (y + 1) * margin]
        low = jnp.concatenate([side, row[:, : half + margin]], axis=1)
        high = jnp.concatenate([row[:, width - half - margin :], side], axis=1)
        lane = y // 2 * stride
        state_ref[y % 2, :, lane : lane + stride] = jnp.where(first, low, high)
    ext_ref[9 * chans :, :] = jnp.zeros((ext_ref.shape[0] - 9 * chans, ext_ref.shape[1]), BF)

    def taken(ref, row, col, start, count):
        lane = row // 2 * stride + col + start
        return ref[row % 2, :, lane : lane + count]

    for s in range(steps):
        n_src = plan.src_rows[s]
        lift, mid = plan.lift[s], plan.mid[s]
        filled = n_src // 2 * stride
        for b in range(2):
            value = state_ref[b, :, :filled]
            if s:
                line = 2 * (3 * s - 1) + b
                value = value * mask_ref[line : line + 1, :filled]
            src_ref[b, :, :filled] = value.astype(BF)
        col = 2 + 4 * s
        for b in range(2):
            for k in range(9):
                i, j = k // 3, k % 3
                ext_ref[k * chans : (k + 1) * chans, b * mid : (b + 1) * mid] = taken(
                    src_ref, b + 1 + i, 1 + j, 0, mid
                )
        for b in range(2):
            line = 6 * s + b
            for base in range(0, lift, TILE):
                window = jnp.concatenate(
                    [taken(src_ref, b + k // 3, k % 3, base, TILE) for k in range(9)], axis=0
                )
                pre = jnp.dot(win_ref[...], window, preferred_element_type=F32)
                keep = mask_ref[line : line + 1, base : base + TILE]
                for q in range(2):
                    val = act(pre, aff_ref[0], aff_ref[col + q])
                    lift_ref[q, b, :, base : base + TILE] = (val * keep).astype(BF)
        pick = index_ref[s]
        ca, cb, cg = table_ref[0, pick], table_ref[1, pick], table_ref[2, pick]
        for q in range(2):
            for bb in range(4):
                for j in range(3):
                    if bb > 1 or j:
                        taps_ref[q, j, :, bb * mid : (bb + 1) * mid] = taken(lift_ref.at[q], bb, j, 0, mid)

        def tap(q, k, base):
            i, j = k // 3, k % 3
            if j:
                return taps_ref[q, j, :, i * mid + base : i * mid + base + TILE]
            parts = []
            for lane in range(i * mid + base, i * mid + base + TILE, 128):
                bb, rest = lane // mid, lane % mid
                parts.append(lift_ref[q, bb, :, rest : rest + 128] if bb < 2 else taps_ref[q, 0, :, lane : lane + 128])
            return jnp.concatenate(parts, axis=1)

        for base in range(0, 2 * mid, TILE):
            vals = []
            for q in range(2):
                window = [tap(q, k, base) for k in range(9)] + [ext_ref[:, base : base + TILE]]
                pre = jnp.dot(wbig_ref[...], jnp.concatenate(window, axis=0), preferred_element_type=F32)
                vals.append(act(pre, aff_ref[1], aff_ref[col + 2 + q]))
            val = vals[0] + cg * (vals[1] - vals[0])
            for part in range(0, TILE, 128):
                b, lane = (base + part) // mid, (base + part) % mid
                line = 6 * s + 2 + b
                keep = mask_ref[line : line + 1, lane : lane + 128]
                low_ref[:, base + part : base + part + 128] = (val[:, part : part + 128] * keep).astype(BF)
        z_ref[:, : 2 * mid] = jnp.dot(wout_ref[...], low_ref[:, : 2 * mid], preferred_element_type=F32)
        done = (n_src - 6) // 2 * stride
        fresh = []
        for b in range(2):
            total = None
            for k in range(9):
                row = b + k // 3
                lane = row % 2 * mid + row // 2 * stride + k % 3
                piece = z_ref[k * chans : (k + 1) * chans, lane : lane + done]
                total = piece if total is None else total + piece
            fresh.append(ca * taken(state_ref, b + 3, 3, 0, done) + cb * total)
        for b in range(2):
            state_ref[b, :, :done] = fresh[b]

    for y in range(plan.rows):
        lane = y // 2 * stride
        out_ref[pl.ds(y, chans, stride=plan.rows), :] = state_ref[y % 2, :, lane : lane + half]


def ring(axis, step):
    count = lax.axis_size(axis)
    return [(i, i + step) for i in range(count) if 0 <= i + step < count]


def shards(latents, in_weight, mid_weight, out_weight, norm_mean, norm_rstd, cond_embed, time_embed,
           time_index, coef_index, sampler_table):
    chans, rows, cols = latents.shape
    feat = mid_weight.shape[2]
    steps = time_index.shape[0]
    half = cols // 2
    plan = Plan(rows, half, steps, chans, feat)
    margin = plan.margin
    cfg = lax.axis_index("cfg")
    swap = [(0, 1), (1, 0)]

    tail = min(rows, ceil_to(margin, 8))
    other = lax.ppermute(cond_embed, "cfg", swap)
    up = lax.ppermute(latents[:, rows - tail :], "band", ring("band", 1)).reshape(chans * tail, cols)
    dn = lax.ppermute(latents[:, :tail], "band", ring("band", -1)).reshape(chans * tail, cols)
    own = latents.reshape(chans * rows, cols)

    times = jnp.concatenate(
        [lax.dynamic_slice_in_dim(time_embed, time_index[i], 1, 0) for i in range(steps)], axis=0
    )
    wbig, win, aff, mask = pl.pallas_call(
        lambda *refs: prep_body(plan, ("band", "sub", "cfg"), *refs),
        out_shape=[
            jax.ShapeDtypeStruct((feat, plan.depth), BF),
            jax.ShapeDtypeStruct((feat, 9 * chans), BF),
            jax.ShapeDtypeStruct((2 + 4 * steps, feat, 128), F32),
            jax.ShapeDtypeStruct((2 * plan.levels, plan.block), F32),
        ],
        in_specs=[VMEM] * 7,
        out_specs=[VMEM] * 4,
        scratch_shapes=[pltpu.VMEM((128, ceil_to(feat, 128)), F32)],
        compiler_params=SMALL,
        name="prep",
    )(times, cond_embed, other, norm_mean, norm_rstd,
      mid_weight.reshape(9 * feat, feat), in_weight.reshape(9 * chans, feat))

    strip = pl.pallas_call(
        lambda *refs: pack_body(plan, tail, "cfg", *refs),
        out_shape=jax.ShapeDtypeStruct((chans, ceil_to(plan.span * margin, 128)), F32),
        in_specs=[VMEM] * 3 + [HBM],
        out_specs=VMEM,
        compiler_params=SMALL,
        name="pack",
    )(up, own, dn, mask)
    subs = lax.axis_size("sub")
    pairs = []
    for i in range(subs - 1):
        pairs += [(2 * i + 1, 2 * i + 2), (2 * i + 2, 2 * i + 1)]
    side = lax.ppermute(strip, ("sub", "cfg"), pairs)

    lift, mid = max(plan.lift), max(plan.mid)
    mine = pl.pallas_call(
        lambda *refs: main_body(plan, tail, "cfg", *refs),
        out_shape=jax.ShapeDtypeStruct((chans * rows, half), F32),
        in_specs=[SMEM, SMEM] + [VMEM] * 9,
        out_specs=VMEM,
        scratch_shapes=[
            pltpu.VMEM((2, chans, plan.block), F32),
            pltpu.VMEM((2, chans, plan.block), BF),
            pltpu.VMEM((2, 2, feat, lift), BF),
            pltpu.VMEM((2, 3, feat, 4 * mid), BF),
            pltpu.VMEM((plan.depth - plan.taps, 2 * mid), BF),
            pltpu.VMEM((feat, 2 * mid), BF),
            pltpu.VMEM((9 * chans, 2 * mid + 128), F32),
        ],
        compiler_params=PARAMS,
        name="denoise",
    )(coef_index, sampler_table, own, up, dn, side, wbig, win, out_weight.reshape(9 * chans, feat), aff, mask)
    theirs = lax.ppermute(mine, "cfg", swap)
    whole = jnp.where(
        cfg == 0, jnp.concatenate([mine, theirs], axis=1), jnp.concatenate([theirs, mine], axis=1)
    )
    return whole.reshape(chans, rows, cols)


def solution(mesh):
    return jax.shard_map(
        shards,
        mesh=mesh,
        in_specs=(P("groups", "band", "sub"), P(), P(), P(), P(), P(), P("cfg", "groups"), P(), P(), P(), P()),
        out_specs=P("groups", "band", "sub"),
        check_vma=False,
    )
```

```python
import jax
import jax.numpy as jnp
from jax import lax
from jax.experimental import pallas as pl
from jax.experimental.pallas import tpu as pltpu
from jax.sharding import PartitionSpec as P

TILE = 256
BF = jnp.bfloat16
F32 = jnp.float32
VMEM = pl.BlockSpec(memory_space=pltpu.VMEM)
SMEM = pl.BlockSpec(memory_space=pltpu.SMEM)
HBM = pl.BlockSpec(memory_space=pltpu.HBM)
PARAMS = pltpu.CompilerParams(vmem_limit_bytes=40 * 1024 * 1024)
LARGE = pltpu.CompilerParams(vmem_limit_bytes=57 * 1024 * 1024)
SMALL = pltpu.CompilerParams(vmem_limit_bytes=8 * 1024 * 1024)


def ceil_to(value, unit):
    return -(-value // unit) * unit


class Plan:
    def __init__(self, rows, half, steps, chans, feat):
        self.rows, self.half, self.steps = rows, half, steps
        self.chans, self.feat = chans, feat
        self.margin = 3 * steps
        self.span = rows + 2 * self.margin
        self.stride = half + 2 * self.margin
        self.src_rows = [self.span - 6 * s for s in range(steps)]
        self.lift = [ceil_to((r - 2) // 2 * self.stride, TILE) for r in self.src_rows]
        self.mid = [ceil_to((r - 4) // 2 * self.stride, 128) for r in self.src_rows]
        self.lift = [
            max(a, ceil_to(b + self.stride + 2, TILE)) for a, b in zip(self.lift, self.mid)
        ]
        self.block = ceil_to(max(self.lift) + 3 * self.stride + 4, 128)
        self.taps = 9 * feat
        self.depth = ceil_to(9 * (feat + chans), 128)
        self.levels = 3 * steps


def act(pre, scale, shift):
    scale = jnp.concatenate([scale] * (pre.shape[1] // 128), axis=1)
    shift = jnp.concatenate([shift] * (pre.shape[1] // 128), axis=1)
    u = pre * scale + shift
    return u + u * jnp.tanh(u)


def prep_body(plan, names, time_ref, other_ref, tail_ref, own_hbm, table_hbm, mean_hbm, rstd_hbm, mid_hbm, in_hbm,
              wbig_ref, win_ref, aff_ref, mask_ref,
              own_ref, block_ref, mean_ref, rstd_ref, mid_ref, in_ref, rows_ref, sem, tap_sem, time_sem):
    feat, chans, steps, stride = plan.feat, plan.chans, plan.steps, plan.stride
    band, sub, cfg = names
    depth = table_hbm.shape[1]
    last = depth // 128 * 128

    blocks = []
    for s in range(steps):
        start = pl.multiple_of(jnp.minimum(time_ref[s] // 128, last // 128 - 1) * 128, 128)
        blocks.append(pltpu.make_async_copy(table_hbm.at[:, pl.ds(start, 128)], block_ref.at[s], time_sem.at[s]))
        blocks[s].start()
    small = [
        pltpu.make_async_copy(src, dst, sem.at[i])
        for i, (src, dst) in enumerate(
            [(in_hbm, in_ref), (own_hbm, own_ref), (mean_hbm, mean_ref), (rstd_hbm, rstd_ref)]
        )
    ]
    for copy in small:
        copy.start()
    taps = [
        pltpu.make_async_copy(mid_hbm.at[pl.ds(k * feat, feat)], mid_ref.at[pl.ds(k * feat, feat)], tap_sem.at[k])
        for k in range(9)
    ]
    for copy in taps:
        copy.start()

    flat = lax.broadcasted_iota(jnp.int32, (8, plan.block), 1)
    ys = jnp.floor((flat.astype(F32) + 0.5) * (1.0 / stride)).astype(jnp.int32)
    xs = flat - ys * stride
    top = lax.axis_index(band) * plan.rows
    left = (lax.axis_index(sub) * 2 + lax.axis_index(cfg)) * plan.half
    height = plan.rows * lax.axis_size(band)
    breadth = 2 * plan.half * lax.axis_size(sub)
    for level in range(plan.levels):
        edge = plan.margin - 1 - level
        gx = xs + (left - edge)
        inx = (gx >= 0) & (gx < breadth)
        for b in range(2):
            gy = 2 * ys + (top - edge + b)
            keep = inx & (gy >= 0) & (gy < height)
            line = 2 * level + b
            mask_ref[line : line + 1, :] = jnp.where(keep, 1.0, 0.0)[0:1, :]

    for copy in small:
        copy.wait()
    turned = jnp.transpose(in_ref[...].astype(F32)).astype(BF)
    win_ref[...] = turned
    wbig_ref[:, plan.taps : plan.taps + 9 * chans] = turned
    rest = plan.depth - 9 * (feat + chans)
    if rest:
        wbig_ref[:, plan.depth - rest :] = jnp.zeros((feat, rest), BF)

    plain = lax.axis_index(cfg) == 0
    rows_ref[...] = jnp.zeros(rows_ref.shape, F32)
    rows_ref[0:2, :feat] = mean_ref[...]
    rows_ref[2:4, :feat] = 0.5 * rstd_ref[...]
    rows_ref[4:5, :feat] = jnp.where(plain, own_ref[...], other_ref[...])
    rows_ref[5:6, :feat] = jnp.where(plain, other_ref[...], own_ref[...])
    turned = jnp.transpose(rows_ref[...])[:feat, :]
    wide = [jnp.broadcast_to(turned[:, i : i + 1], (feat, 128)) for i in range(6)]
    aff_ref[0] = wide[2]
    aff_ref[1] = wide[3]
    lanes = lax.broadcasted_iota(jnp.int32, (feat, 128), 1)
    for s in range(steps):
        blocks[s].wait()
        block = jnp.where(time_ref[s] < last, block_ref[s], tail_ref[...])
        time = jnp.sum(jnp.where(lanes == time_ref[s] % 128, block, 0.0), axis=1, keepdims=True)
        time = jnp.broadcast_to(time, (feat, 128))
        for k in range(2):
            for q in range(2):
                aff_ref[2 + 4 * s + 2 * k + q] = (time + wide[4 + q] - wide[k]) * wide[2 + k]
    for k in range(9):
        taps[k].wait()
        wbig_ref[:, k * feat : (k + 1) * feat] = mid_ref[k * feat : (k + 1) * feat, :]


def field_row(plan, y, up_ref, own_ref, dn_ref, tail):
    if y < plan.margin:
        return up_ref[pl.ds(tail - plan.margin + y, plan.chans, stride=tail), :]
    if y < plan.margin + plan.rows:
        return own_ref[pl.ds(y - plan.margin, plan.chans, stride=plan.rows), :]
    return dn_ref[pl.ds(y - plan.margin - plan.rows, plan.chans, stride=tail), :]


def pack_body(plan, tail, cfg, up_ref, own_ref, dn_ref, after_ref, out_ref):
    del after_ref
    right = lax.axis_index(cfg) == 1
    width, margin = own_ref.shape[1], plan.margin
    for y in range(plan.span):
        row = field_row(plan, y, up_ref, own_ref, dn_ref, tail)
        out_ref[:, y * margin : (y + 1) * margin] = jnp.where(right, row[:, width - margin :], row[:, :margin])


def main_body(plan, tail, cfg, index_ref, table_ref, own_ref, up_ref, dn_ref, side_ref, wbig_ref, win_ref, wout_ref,
              aff_ref, mask_ref, out_ref, state_ref, src_ref, lift_ref, taps_ref, ext_ref, low_ref, z_ref):
    stride, chans, feat, steps = plan.stride, plan.chans, plan.feat, plan.steps
    margin, half = plan.margin, plan.half
    first = lax.axis_index(cfg) == 0
    width = own_ref.shape[1]

    for y in range(plan.span):
        row = field_row(plan, y, up_ref, own_ref, dn_ref, tail)
        side = side_ref[:, y * margin : (y + 1) * margin]
        low = jnp.concatenate([side, row[:, : half + margin]], axis=1)
        high = jnp.concatenate([row[:, width - half - margin :], side], axis=1)
        lane = y // 2 * stride
        state_ref[y % 2, :, lane : lane + stride] = jnp.where(first, low, high)
    ext_ref[9 * chans :, :] = jnp.zeros((ext_ref.shape[0] - 9 * chans, ext_ref.shape[1]), BF)

    def taken(ref, row, col, start, count):
        lane = row // 2 * stride + col + start
        return ref[row % 2, :, lane : lane + count]

    for s in range(steps):
        n_src = plan.src_rows[s]
        lift, mid = plan.lift[s], plan.mid[s]
        filled = n_src // 2 * stride
        for b in range(2):
            value = state_ref[b, :, :filled]
            if s:
                line = 2 * (3 * s - 1) + b
                value = value * mask_ref[line : line + 1, :filled]
            src_ref[b, :, :filled] = value.astype(BF)
        col = 2 + 4 * s
        for b in range(2):
            for k in range(9):
                i, j = k // 3, k % 3
                ext_ref[k * chans : (k + 1) * chans, b * mid : (b + 1) * mid] = taken(
                    src_ref, b + 1 + i, 1 + j, 0, mid
                )
        for b in range(2):
            line = 6 * s + b
            for base in range(0, lift, TILE):
                window = jnp.concatenate(
                    [taken(src_ref, b + k // 3, k % 3, base, TILE) for k in range(9)], axis=0
                )
                pre = jnp.dot(win_ref[...], window, preferred_element_type=F32)
                keep = mask_ref[line : line + 1, base : base + TILE]
                for q in range(2):
                    val = act(pre, aff_ref[0], aff_ref[col + q])
                    lift_ref[q, b, :, base : base + TILE] = (val * keep).astype(BF)
        pick = index_ref[s]
        ca, cb, cg = table_ref[0, pick], table_ref[1, pick], table_ref[2, pick]
        for q in range(2):
            for bb in range(4):
                for j in range(3):
                    if bb > 1 or j:
                        taps_ref[q, j, :, bb * mid : (bb + 1) * mid] = taken(lift_ref.at[q], bb, j, 0, mid)

        def tap(q, k, base):
            i, j = k // 3, k % 3
            if j:
                return taps_ref[q, j, :, i * mid + base : i * mid + base + TILE]
            parts = []
            for lane in range(i * mid + base, i * mid + base + TILE, 128):
                bb, rest = lane // mid, lane % mid
                parts.append(lift_ref[q, bb, :, rest : rest + 128] if bb < 2 else taps_ref[q, 0, :, lane : lane + 128])
            return jnp.concatenate(parts, axis=1)

        for base in range(0, 2 * mid, TILE):
            vals = []
            for q in range(2):
                window = [tap(q, k, base) for k in range(9)] + [ext_ref[:, base : base + TILE]]
                pre = jnp.dot(wbig_ref[...], jnp.concatenate(window, axis=0), preferred_element_type=F32)
                vals.append(act(pre, aff_ref[1], aff_ref[col + 2 + q]))
            val = vals[0] + cg * (vals[1] - vals[0])
            for part in range(0, TILE, 128):
                b, lane = (base + part) // mid, (base + part) % mid
                line = 6 * s + 2 + b
                keep = mask_ref[line : line + 1, lane : lane + 128]
                low_ref[:, base + part : base + part + 128] = (val[:, part : part + 128] * keep).astype(BF)
        z_ref[:, : 2 * mid] = jnp.dot(wout_ref[...], low_ref[:, : 2 * mid], preferred_element_type=F32)
        done = (n_src - 6) // 2 * stride
        fresh = []
        for b in range(2):
            total = None
            for k in range(9):
                row = b + k // 3
                lane = row % 2 * mid + row // 2 * stride + k % 3
                piece = z_ref[k * chans : (k + 1) * chans, lane : lane + done]
                total = piece if total is None else total + piece
            fresh.append(ca * taken(state_ref, b + 3, 3, 0, done) + cb * total)
        for b in range(2):
            state_ref[b, :, :done] = fresh[b]

    for y in range(plan.rows):
        lane = y // 2 * stride
        out_ref[pl.ds(y, chans, stride=plan.rows), :] = state_ref[y % 2, :, lane : lane + half]


def ring(axis, step):
    count = lax.axis_size(axis)
    return [(i, i + step) for i in range(count) if 0 <= i + step < count]


def shards(latents, in_weight, mid_weight, out_weight, norm_mean, norm_rstd, cond_embed, time_embed,
           time_index, coef_index, sampler_table):
    chans, rows, cols = latents.shape
    feat = mid_weight.shape[2]
    steps = time_index.shape[0]
    half = cols // 2
    plan = Plan(rows, half, steps, chans, feat)
    margin = plan.margin
    cfg = lax.axis_index("cfg")
    swap = [(0, 1), (1, 0)]

    tail = min(rows, ceil_to(margin, 8))
    other = lax.ppermute(cond_embed, "cfg", swap)
    up = lax.ppermute(latents[:, rows - tail :], "band", ring("band", 1)).reshape(chans * tail, cols)
    dn = lax.ppermute(latents[:, :tail], "band", ring("band", -1)).reshape(chans * tail, cols)
    own = latents.reshape(chans * rows, cols)

    table = time_embed.T
    ends = table[:, table.shape[1] // 128 * 128 :]
    ends = jnp.pad(ends, ((0, 0), (0, 128 - ends.shape[1])))
    wbig, win, aff, mask = pl.pallas_call(
        lambda *refs: prep_body(plan, ("band", "sub", "cfg"), *refs),
        out_shape=[
            jax.ShapeDtypeStruct((feat, plan.depth), BF),
            jax.ShapeDtypeStruct((feat, 9 * chans), BF),
            jax.ShapeDtypeStruct((2 + 4 * steps, feat, 128), F32),
            jax.ShapeDtypeStruct((2 * plan.levels, plan.block), F32),
        ],
        in_specs=[SMEM, VMEM, VMEM] + [HBM] * 6,
        out_specs=[VMEM] * 4,
        scratch_shapes=[
            pltpu.VMEM((1, feat), F32),
            pltpu.VMEM((steps, feat, 128), F32),
            pltpu.VMEM((2, feat), F32),
            pltpu.VMEM((2, feat), F32),
            pltpu.VMEM((9 * feat, feat), BF),
            pltpu.VMEM((9 * chans, feat), BF),
            pltpu.VMEM((128, ceil_to(feat, 128)), F32),
            pltpu.SemaphoreType.DMA((4,)),
            pltpu.SemaphoreType.DMA((9,)),
            pltpu.SemaphoreType.DMA((steps,)),
        ],
        compiler_params=LARGE,
        name="prep",
    )(time_index, other, ends, cond_embed, table, norm_mean, norm_rstd,
      mid_weight.reshape(9 * feat, feat), in_weight.reshape(9 * chans, feat))

    strip = pl.pallas_call(
        lambda *refs: pack_body(plan, tail, "cfg", *refs),
        out_shape=jax.ShapeDtypeStruct((chans, ceil_to(plan.span * margin, 128)), F32),
        in_specs=[VMEM] * 3 + [pl.BlockSpec(memory_space=pl.ANY)],
        out_specs=VMEM,
        compiler_params=SMALL,
        name="pack",
    )(up, own, dn, mask)
    subs = lax.axis_size("sub")
    pairs = []
    for i in range(subs - 1):
        pairs += [(2 * i + 1, 2 * i + 2), (2 * i + 2, 2 * i + 1)]
    side = lax.ppermute(strip, ("sub", "cfg"), pairs)

    lift, mid = max(plan.lift), max(plan.mid)
    mine = pl.pallas_call(
        lambda *refs: main_body(plan, tail, "cfg", *refs),
        out_shape=jax.ShapeDtypeStruct((chans * rows, half), F32),
        in_specs=[SMEM, SMEM] + [VMEM] * 9,
        out_specs=VMEM,
        scratch_shapes=[
            pltpu.VMEM((2, chans, plan.block), F32),
            pltpu.VMEM((2, chans, plan.block), BF),
            pltpu.VMEM((2, 2, feat, lift), BF),
            pltpu.VMEM((2, 3, feat, 4 * mid), BF),
            pltpu.VMEM((plan.depth - plan.taps, 2 * mid), BF),
            pltpu.VMEM((feat, 2 * mid), BF),
            pltpu.VMEM((9 * chans, 2 * mid + 128), F32),
        ],
        compiler_params=PARAMS,
        name="denoise",
    )(coef_index, sampler_table, own, up, dn, side, wbig, win, out_weight.reshape(9 * chans, feat), aff, mask)
    theirs = lax.ppermute(mine, "cfg", swap)
    whole = jnp.where(
        cfg == 0, jnp.concatenate([mine, theirs], axis=1), jnp.concatenate([theirs, mine], axis=1)
    )
    return whole.reshape(chans, rows, cols)


def solution(mesh):
    return jax.shard_map(
        shards,
        mesh=mesh,
        in_specs=(P("groups", "band", "sub"), P(), P(), P(), P(), P(), P("cfg", "groups"), P(), P(), P(), P()),
        out_specs=P("groups", "band", "sub"),
        check_vma=False,
    )
```

```python
import jax
import jax.numpy as jnp
from jax import lax
from jax.experimental import pallas as pl
from jax.experimental.pallas import tpu as pltpu
from jax.sharding import PartitionSpec as P

TILE = 256
BF = jnp.bfloat16
F32 = jnp.float32
VMEM = pl.BlockSpec(memory_space=pltpu.VMEM)
SMEM = pl.BlockSpec(memory_space=pltpu.SMEM)
PARAMS = pltpu.CompilerParams(vmem_limit_bytes=40 * 1024 * 1024)
SMALL = pltpu.CompilerParams(vmem_limit_bytes=8 * 1024 * 1024)


def ceil_to(value, unit):
    return -(-value // unit) * unit


class Plan:
    def __init__(self, rows, half, steps, chans, feat):
        self.rows, self.half, self.steps = rows, half, steps
        self.chans, self.feat = chans, feat
        self.margin = 3 * steps
        self.span = rows + 2 * self.margin
        self.stride = half + 2 * self.margin
        self.src_rows = [self.span - 6 * s for s in range(steps)]
        self.lift = [ceil_to((r - 2) // 2 * self.stride, TILE) for r in self.src_rows]
        self.mid = [ceil_to((r - 4) // 2 * self.stride, 128) for r in self.src_rows]
        self.lift = [
            max(a, ceil_to(b + self.stride + 2, TILE)) for a, b in zip(self.lift, self.mid)
        ]
        self.block = ceil_to(max(self.lift) + 3 * self.stride + 4, 128)
        self.taps = 9 * feat
        self.depth = ceil_to(9 * (feat + chans), 128)
        self.levels = 3 * steps


def act(pre, scale, shift):
    scale = jnp.concatenate([scale] * (pre.shape[1] // 128), axis=1)
    shift = jnp.concatenate([shift] * (pre.shape[1] // 128), axis=1)
    u = pre * scale + shift
    return u + u * jnp.tanh(u)


def prep_body(plan, names, time_ref, other_ref, own_ref, table_ref, mean_ref, rstd_ref, mid_ref, in_ref, after_ref,
              wbig_ref, win_ref, aff_ref, mask_ref, rows_ref):
    del after_ref
    feat, chans, steps, stride = plan.feat, plan.chans, plan.steps, plan.stride
    band, sub, cfg = names
    depth = table_ref.shape[1]
    last = depth // 128 * 128
    for k in range(9):
        wbig_ref[:, k * feat : (k + 1) * feat] = mid_ref[k * feat : (k + 1) * feat, :]

    flat = lax.broadcasted_iota(jnp.int32, (8, plan.block), 1)
    ys = jnp.floor((flat.astype(F32) + 0.5) * (1.0 / stride)).astype(jnp.int32)
    xs = flat - ys * stride
    top = lax.axis_index(band) * plan.rows
    left = (lax.axis_index(sub) * 2 + lax.axis_index(cfg)) * plan.half
    height = plan.rows * lax.axis_size(band)
    breadth = 2 * plan.half * lax.axis_size(sub)
    for level in range(plan.levels):
        edge = plan.margin - 1 - level
        gx = xs + (left - edge)
        inx = (gx >= 0) & (gx < breadth)
        for b in range(2):
            gy = 2 * ys + (top - edge + b)
            keep = inx & (gy >= 0) & (gy < height)
            line = 2 * level + b
            mask_ref[line : line + 1, :] = jnp.where(keep, 1.0, 0.0)[0:1, :]

    turned = jnp.transpose(in_ref[...].astype(F32)).astype(BF)
    win_ref[...] = turned
    wbig_ref[:, plan.taps : plan.taps + 9 * chans] = turned
    rest = plan.depth - 9 * (feat + chans)
    if rest:
        wbig_ref[:, plan.depth - rest :] = jnp.zeros((feat, rest), BF)

    plain = lax.axis_index(cfg) == 0
    rows_ref[...] = jnp.zeros(rows_ref.shape, F32)
    rows_ref[0:2, :feat] = mean_ref[...]
    rows_ref[2:4, :feat] = 0.5 * rstd_ref[...]
    rows_ref[4:5, :feat] = jnp.where(plain, own_ref[...], other_ref[...])
    rows_ref[5:6, :feat] = jnp.where(plain, other_ref[...], own_ref[...])
    turned = jnp.transpose(rows_ref[...])[:feat, :]
    wide = [jnp.broadcast_to(turned[:, i : i + 1], (feat, 128)) for i in range(6)]
    aff_ref[0] = wide[2]
    aff_ref[1] = wide[3]
    lanes = lax.broadcasted_iota(jnp.int32, (feat, 128), 1)
    for s in range(steps):
        start = pl.multiple_of(jnp.minimum(time_ref[s] // 128, last // 128 - 1) * 128, 128)
        block = table_ref[:, pl.ds(start, 128)]
        if last < depth:
            end = jnp.concatenate([table_ref[:, last:], jnp.zeros((feat, last + 128 - depth), F32)], axis=1)
            block = jnp.where(time_ref[s] < last, block, end)
        time = jnp.sum(jnp.where(lanes == time_ref[s] % 128, block, 0.0), axis=1, keepdims=True)
        time = jnp.broadcast_to(time, (feat, 128))
        for k in range(2):
            for q in range(2):
                aff_ref[2 + 4 * s + 2 * k + q] = (time + wide[4 + q] - wide[k]) * wide[2 + k]


def field_row(plan, y, up_ref, own_ref, dn_ref, tail):
    if y < plan.margin:
        return up_ref[pl.ds(tail - plan.margin + y, plan.chans, stride=tail), :]
    if y < plan.margin + plan.rows:
        return own_ref[pl.ds(y - plan.margin, plan.chans, stride=plan.rows), :]
    return dn_ref[pl.ds(y - plan.margin - plan.rows, plan.chans, stride=tail), :]


def pack_body(plan, tail, cfg, up_ref, own_ref, dn_ref, out_ref):
    right = lax.axis_index(cfg) == 1
    width, margin = own_ref.shape[1], plan.margin
    for y in range(plan.span):
        row = field_row(plan, y, up_ref, own_ref, dn_ref, tail)
        out_ref[:, y * margin : (y + 1) * margin] = jnp.where(right, row[:, width - margin :], row[:, :margin])


def main_body(plan, tail, cfg, index_ref, table_ref, own_ref, up_ref, dn_ref, side_ref, wbig_ref, win_ref, wout_ref,
              aff_ref, mask_ref, out_ref, state_ref, src_ref, lift_ref, taps_ref, ext_ref, low_ref, z_ref):
    stride, chans, feat, steps = plan.stride, plan.chans, plan.feat, plan.steps
    margin, half = plan.margin, plan.half
    first = lax.axis_index(cfg) == 0
    width = own_ref.shape[1]

    for y in range(plan.span):
        row = field_row(plan, y, up_ref, own_ref, dn_ref, tail)
        side = side_ref[:, y * margin : (y + 1) * margin]
        low = jnp.concatenate([side, row[:, : half + margin]], axis=1)
        high = jnp.concatenate([row[:, width - half - margin :], side], axis=1)
        lane = y // 2 * stride
        state_ref[y % 2, :, lane : lane + stride] = jnp.where(first, low, high)
    ext_ref[9 * chans :, :] = jnp.zeros((ext_ref.shape[0] - 9 * chans, ext_ref.shape[1]), BF)

    def taken(ref, row, col, start, count):
        lane = row // 2 * stride + col + start
        return ref[row % 2, :, lane : lane + count]

    for s in range(steps):
        n_src = plan.src_rows[s]
        lift, mid = plan.lift[s], plan.mid[s]
        filled = n_src // 2 * stride
        for b in range(2):
            value = state_ref[b, :, :filled]
            if s:
                line = 2 * (3 * s - 1) + b
                value = value * mask_ref[line : line + 1, :filled]
            src_ref[b, :, :filled] = value.astype(BF)
        col = 2 + 4 * s
        for b in range(2):
            for k in range(9):
                i, j = k // 3, k % 3
                ext_ref[k * chans : (k + 1) * chans, b * mid : (b + 1) * mid] = taken(
                    src_ref, b + 1 + i, 1 + j, 0, mid
                )
        for b in range(2):
            line = 6 * s + b
            for base in range(0, lift, TILE):
                window = jnp.concatenate(
                    [taken(src_ref, b + k // 3, k % 3, base, TILE) for k in range(9)], axis=0
                )
                pre = jnp.dot(win_ref[...], window, preferred_element_type=F32)
                keep = mask_ref[line : line + 1, base : base + TILE]
                for q in range(2):
                    val = act(pre, aff_ref[0], aff_ref[col + q])
                    lift_ref[q, b, :, base : base + TILE] = (val * keep).astype(BF)
        pick = index_ref[s]
        ca, cb, cg = table_ref[0, pick], table_ref[1, pick], table_ref[2, pick]
        for q in range(2):
            for bb in range(4):
                for j in range(3):
                    if bb > 1 or j:
                        taps_ref[q, j, :, bb * mid : (bb + 1) * mid] = taken(lift_ref.at[q], bb, j, 0, mid)

        def tap(q, k, base):
            i, j = k // 3, k % 3
            if j:
                return taps_ref[q, j, :, i * mid + base : i * mid + base + TILE]
            parts = []
            for lane in range(i * mid + base, i * mid + base + TILE, 128):
                bb, rest = lane // mid, lane % mid
                parts.append(lift_ref[q, bb, :, rest : rest + 128] if bb < 2 else taps_ref[q, 0, :, lane : lane + 128])
            return jnp.concatenate(parts, axis=1)

        for base in range(0, 2 * mid, TILE):
            vals = []
            for q in range(2):
                window = [tap(q, k, base) for k in range(9)] + [ext_ref[:, base : base + TILE]]
                pre = jnp.dot(wbig_ref[...], jnp.concatenate(window, axis=0), preferred_element_type=F32)
                vals.append(act(pre, aff_ref[1], aff_ref[col + 2 + q]))
            val = vals[0] + cg * (vals[1] - vals[0])
            for part in range(0, TILE, 128):
                b, lane = (base + part) // mid, (base + part) % mid
                line = 6 * s + 2 + b
                keep = mask_ref[line : line + 1, lane : lane + 128]
                low_ref[:, base + part : base + part + 128] = (val[:, part : part + 128] * keep).astype(BF)
        z_ref[:, : 2 * mid] = jnp.dot(wout_ref[...], low_ref[:, : 2 * mid], preferred_element_type=F32)
        done = (n_src - 6) // 2 * stride
        fresh = []
        for b in range(2):
            total = None
            for k in range(9):
                row = b + k // 3
                lane = row % 2 * mid + row // 2 * stride + k % 3
                piece = z_ref[k * chans : (k + 1) * chans, lane : lane + done]
                total = piece if total is None else total + piece
            fresh.append(ca * taken(state_ref, b + 3, 3, 0, done) + cb * total)
        for b in range(2):
            state_ref[b, :, :done] = fresh[b]

    for y in range(plan.rows):
        lane = y // 2 * stride
        out_ref[pl.ds(y, chans, stride=plan.rows), :] = state_ref[y % 2, :, lane : lane + half]


def ring(axis, step):
    count = lax.axis_size(axis)
    return [(i, i + step) for i in range(count) if 0 <= i + step < count]


def shards(latents, in_weight, mid_weight, out_weight, norm_mean, norm_rstd, cond_embed, time_embed,
           time_index, coef_index, sampler_table):
    chans, rows, cols = latents.shape
    feat = mid_weight.shape[2]
    steps = time_index.shape[0]
    half = cols // 2
    plan = Plan(rows, half, steps, chans, feat)
    margin = plan.margin
    cfg = lax.axis_index("cfg")
    swap = [(0, 1), (1, 0)]

    tail = min(rows, ceil_to(margin, 8))
    other = lax.ppermute(cond_embed, "cfg", swap)
    up = lax.ppermute(latents[:, rows - tail :], "band", ring("band", 1)).reshape(chans * tail, cols)
    dn = lax.ppermute(latents[:, :tail], "band", ring("band", -1)).reshape(chans * tail, cols)
    own = latents.reshape(chans * rows, cols)

    strip = pl.pallas_call(
        lambda *refs: pack_body(plan, tail, "cfg", *refs),
        out_shape=jax.ShapeDtypeStruct((chans, ceil_to(plan.span * margin, 128)), F32),
        in_specs=[VMEM] * 3,
        out_specs=VMEM,
        compiler_params=SMALL,
        cost_estimate=pl.CostEstimate(flops=8_000_000_000, transcendentals=0, bytes_accessed=200_000),
        name="pack",
    )(up, own, dn)
    subs = lax.axis_size("sub")
    pairs = []
    for i in range(subs - 1):
        pairs += [(2 * i + 1, 2 * i + 2), (2 * i + 2, 2 * i + 1)]
    side = lax.ppermute(strip, ("sub", "cfg"), pairs)

    wbig, win, aff, mask = pl.pallas_call(
        lambda *refs: prep_body(plan, ("band", "sub", "cfg"), *refs),
        out_shape=[
            jax.ShapeDtypeStruct((feat, plan.depth), BF),
            jax.ShapeDtypeStruct((feat, 9 * chans), BF),
            jax.ShapeDtypeStruct((2 + 4 * steps, feat, 128), F32),
            jax.ShapeDtypeStruct((2 * plan.levels, plan.block), F32),
        ],
        in_specs=[SMEM] + [VMEM] * 8,
        out_specs=[VMEM] * 4,
        scratch_shapes=[pltpu.VMEM((128, ceil_to(feat, 128)), F32)],
        compiler_params=SMALL,
        name="prep",
    )(time_index, other, cond_embed, time_embed.T, norm_mean, norm_rstd,
      mid_weight.reshape(9 * feat, feat), in_weight.reshape(9 * chans, feat), strip)

    lift, mid = max(plan.lift), max(plan.mid)
    mine = pl.pallas_call(
        lambda *refs: main_body(plan, tail, "cfg", *refs),
        out_shape=jax.ShapeDtypeStruct((chans * rows, half), F32),
        in_specs=[SMEM, SMEM] + [VMEM] * 9,
        out_specs=VMEM,
        scratch_shapes=[
            pltpu.VMEM((2, chans, plan.block), F32),
            pltpu.VMEM((2, chans, plan.block), BF),
            pltpu.VMEM((2, 2, feat, lift), BF),
            pltpu.VMEM((2, 3, feat, 4 * mid), BF),
            pltpu.VMEM((plan.depth - plan.taps, 2 * mid), BF),
            pltpu.VMEM((feat, 2 * mid), BF),
            pltpu.VMEM((9 * chans, 2 * mid + 128), F32),
        ],
        compiler_params=PARAMS,
        name="denoise",
    )(coef_index, sampler_table, own, up, dn, side, wbig, win, out_weight.reshape(9 * chans, feat), aff, mask)
    theirs = lax.ppermute(mine, "cfg", swap)
    whole = jnp.where(
        cfg == 0, jnp.concatenate([mine, theirs], axis=1), jnp.concatenate([theirs, mine], axis=1)
    )
    return whole.reshape(chans, rows, cols)


def solution(mesh):
    return jax.shard_map(
        shards,
        mesh=mesh,
        in_specs=(P("groups", "band", "sub"), P(), P(), P(), P(), P(), P("cfg", "groups"), P(), P(), P(), P()),
        out_specs=P("groups", "band", "sub"),
        check_vma=False,
    )
```

```python
import jax
import jax.numpy as jnp
from jax import lax
from jax.experimental import pallas as pl
from jax.experimental.pallas import tpu as pltpu
from jax.sharding import PartitionSpec as P

TILE = 256
BF = jnp.bfloat16
F32 = jnp.float32
ANY = pl.BlockSpec(memory_space=pl.ANY)
VMEM = pl.BlockSpec(memory_space=pltpu.VMEM)
SMEM = pl.BlockSpec(memory_space=pltpu.SMEM)
PARAMS = pltpu.CompilerParams(vmem_limit_bytes=40 * 1024 * 1024)
SMALL = pltpu.CompilerParams(vmem_limit_bytes=8 * 1024 * 1024)


def ceil_to(value, unit):
    return -(-value // unit) * unit


class Plan:
    def __init__(self, rows, half, steps, chans, feat):
        self.rows, self.half, self.steps = rows, half, steps
        self.chans, self.feat = chans, feat
        self.margin = 3 * steps
        self.span = rows + 2 * self.margin
        self.stride = half + 2 * self.margin
        self.src_rows = [self.span - 6 * s for s in range(steps)]
        self.lift = [ceil_to((r - 2) // 2 * self.stride, TILE) for r in self.src_rows]
        self.mid = [ceil_to((r - 4) // 2 * self.stride, 128) for r in self.src_rows]
        self.lift = [
            max(a, ceil_to(b + self.stride + 2, TILE)) for a, b in zip(self.lift, self.mid)
        ]
        self.block = ceil_to(max(self.lift) + 3 * self.stride + 4, 128)
        self.taps = 9 * feat
        self.depth = ceil_to(9 * (feat + chans), 128)
        self.levels = 3 * steps


def act(pre, scale, shift):
    scale = jnp.concatenate([scale] * (pre.shape[1] // 128), axis=1)
    shift = jnp.concatenate([shift] * (pre.shape[1] // 128), axis=1)
    u = pre * scale + shift
    return u + u * jnp.tanh(u)


def mask_body(plan, names, mask_ref):
    stride = plan.stride
    band, sub, cfg = names
    flat = lax.broadcasted_iota(jnp.int32, (8, plan.block), 1)
    ys = jnp.floor((flat.astype(F32) + 0.5) * (1.0 / stride)).astype(jnp.int32)
    xs = flat - ys * stride
    top = lax.axis_index(band) * plan.rows
    left = (lax.axis_index(sub) * 2 + lax.axis_index(cfg)) * plan.half
    height = plan.rows * lax.axis_size(band)
    breadth = 2 * plan.half * lax.axis_size(sub)
    for level in range(plan.levels):
        edge = plan.margin - 1 - level
        gx = xs + (left - edge)
        inx = (gx >= 0) & (gx < breadth)
        for b in range(2):
            gy = 2 * ys + (top - edge + b)
            keep = inx & (gy >= 0) & (gy < height)
            line = 2 * level + b
            mask_ref[line : line + 1, :] = jnp.where(keep, 1.0, 0.0)[0:1, :]


def prep_body(plan, cfg, time_ref, other_ref, own_ref, table_ref, mean_ref, rstd_ref, mid_ref, in_ref, after_ref,
              wbig_ref, win_ref, aff_ref, rows_ref):
    del after_ref
    feat, chans, steps = plan.feat, plan.chans, plan.steps
    depth = table_ref.shape[1]
    last = depth // 128 * 128
    for k in range(9):
        wbig_ref[:, k * feat : (k + 1) * feat] = mid_ref[k * feat : (k + 1) * feat, :]

    turned = jnp.transpose(in_ref[...].astype(F32)).astype(BF)
    win_ref[...] = turned
    wbig_ref[:, plan.taps : plan.taps + 9 * chans] = turned
    rest = plan.depth - 9 * (feat + chans)
    if rest:
        wbig_ref[:, plan.depth - rest :] = jnp.zeros((feat, rest), BF)

    plain = lax.axis_index(cfg) == 0
    rows_ref[...] = jnp.zeros(rows_ref.shape, F32)
    rows_ref[0:2, :feat] = mean_ref[...]
    rows_ref[2:4, :feat] = 0.5 * rstd_ref[...]
    rows_ref[4:5, :feat] = jnp.where(plain, own_ref[...], other_ref[...])
    rows_ref[5:6, :feat] = jnp.where(plain, other_ref[...], own_ref[...])
    turned = jnp.transpose(rows_ref[...])[:feat, :]
    wide = [jnp.broadcast_to(turned[:, i : i + 1], (feat, 128)) for i in range(6)]
    aff_ref[0] = wide[2]
    aff_ref[1] = wide[3]
    lanes = lax.broadcasted_iota(jnp.int32, (feat, 128), 1)
    for s in range(steps):
        start = pl.multiple_of(jnp.minimum(time_ref[s] // 128, last // 128 - 1) * 128, 128)
        block = table_ref[:, pl.ds(start, 128)]
        if last < depth:
            end = jnp.concatenate([table_ref[:, last:], jnp.zeros((feat, last + 128 - depth), F32)], axis=1)
            block = jnp.where(time_ref[s] < last, block, end)
        time = jnp.sum(jnp.where(lanes == time_ref[s] % 128, block, 0.0), axis=1, keepdims=True)
        time = jnp.broadcast_to(time, (feat, 128))
        for k in range(2):
            for q in range(2):
                aff_ref[2 + 4 * s + 2 * k + q] = (time + wide[4 + q] - wide[k]) * wide[2 + k]


def field_row(plan, y, up_ref, own_ref, dn_ref, tail):
    if y < plan.margin:
        return up_ref[pl.ds(tail - plan.margin + y, plan.chans, stride=tail), :]
    if y < plan.margin + plan.rows:
        return own_ref[pl.ds(y - plan.margin, plan.chans, stride=plan.rows), :]
    return dn_ref[pl.ds(y - plan.margin - plan.rows, plan.chans, stride=tail), :]


def pack_body(plan, tail, cfg, up_ref, own_ref, dn_ref, after_ref, out_ref):
    del after_ref
    right = lax.axis_index(cfg) == 1
    width, margin = own_ref.shape[1], plan.margin
    for y in range(plan.span):
        row = field_row(plan, y, up_ref, own_ref, dn_ref, tail)
        out_ref[:, y * margin : (y + 1) * margin] = jnp.where(right, row[:, width - margin :], row[:, :margin])


def main_body(plan, tail, cfg, index_ref, table_ref, own_ref, up_ref, dn_ref, side_ref, wbig_ref, win_ref, wout_ref,
              aff_ref, mask_ref, out_ref, state_ref, src_ref, lift_ref, taps_ref, ext_ref, low_ref, z_ref):
    stride, chans, feat, steps = plan.stride, plan.chans, plan.feat, plan.steps
    margin, half = plan.margin, plan.half
    first = lax.axis_index(cfg) == 0
    width = own_ref.shape[1]

    for y in range(plan.span):
        row = field_row(plan, y, up_ref, own_ref, dn_ref, tail)
        side = side_ref[:, y * margin : (y + 1) * margin]
        low = jnp.concatenate([side, row[:, : half + margin]], axis=1)
        high = jnp.concatenate([row[:, width - half - margin :], side], axis=1)
        lane = y // 2 * stride
        state_ref[y % 2, :, lane : lane + stride] = jnp.where(first, low, high)
    ext_ref[9 * chans :, :] = jnp.zeros((ext_ref.shape[0] - 9 * chans, ext_ref.shape[1]), BF)

    def taken(ref, row, col, start, count):
        lane = row // 2 * stride + col + start
        return ref[row % 2, :, lane : lane + count]

    for s in range(steps):
        n_src = plan.src_rows[s]
        lift, mid = plan.lift[s], plan.mid[s]
        filled = n_src // 2 * stride
        for b in range(2):
            value = state_ref[b, :, :filled]
            if s:
                line = 2 * (3 * s - 1) + b
                value = value * mask_ref[line : line + 1, :filled]
            src_ref[b, :, :filled] = value.astype(BF)
        col = 2 + 4 * s
        for b in range(2):
            for k in range(9):
                i, j = k // 3, k % 3
                ext_ref[k * chans : (k + 1) * chans, b * mid : (b + 1) * mid] = taken(
                    src_ref, b + 1 + i, 1 + j, 0, mid
                )
        for b in range(2):
            line = 6 * s + b
            for base in range(0, lift, TILE):
                window = jnp.concatenate(
                    [taken(src_ref, b + k // 3, k % 3, base, TILE) for k in range(9)], axis=0
                )
                pre = jnp.dot(win_ref[...], window, preferred_element_type=F32)
                keep = mask_ref[line : line + 1, base : base + TILE]
                for q in range(2):
                    val = act(pre, aff_ref[0], aff_ref[col + q])
                    lift_ref[q, b, :, base : base + TILE] = (val * keep).astype(BF)
        pick = index_ref[s]
        ca, cb, cg = table_ref[0, pick], table_ref[1, pick], table_ref[2, pick]
        for q in range(2):
            for bb in range(4):
                for j in range(3):
                    if bb > 1 or j:
                        taps_ref[q, j, :, bb * mid : (bb + 1) * mid] = taken(lift_ref.at[q], bb, j, 0, mid)

        def tap(q, k, base):
            i, j = k // 3, k % 3
            if j:
                return taps_ref[q, j, :, i * mid + base : i * mid + base + TILE]
            parts = []
            for lane in range(i * mid + base, i * mid + base + TILE, 128):
                bb, rest = lane // mid, lane % mid
                parts.append(lift_ref[q, bb, :, rest : rest + 128] if bb < 2 else taps_ref[q, 0, :, lane : lane + 128])
            return jnp.concatenate(parts, axis=1)

        for base in range(0, 2 * mid, TILE):
            vals = []
            for q in range(2):
                window = [tap(q, k, base) for k in range(9)] + [ext_ref[:, base : base + TILE]]
                pre = jnp.dot(wbig_ref[...], jnp.concatenate(window, axis=0), preferred_element_type=F32)
                vals.append(act(pre, aff_ref[1], aff_ref[col + 2 + q]))
            val = vals[0] + cg * (vals[1] - vals[0])
            for part in range(0, TILE, 128):
                b, lane = (base + part) // mid, (base + part) % mid
                line = 6 * s + 2 + b
                keep = mask_ref[line : line + 1, lane : lane + 128]
                low_ref[:, base + part : base + part + 128] = (val[:, part : part + 128] * keep).astype(BF)
        z_ref[:, : 2 * mid] = jnp.dot(wout_ref[...], low_ref[:, : 2 * mid], preferred_element_type=F32)
        done = (n_src - 6) // 2 * stride
        fresh = []
        for b in range(2):
            total = None
            for k in range(9):
                row = b + k // 3
                lane = row % 2 * mid + row // 2 * stride + k % 3
                piece = z_ref[k * chans : (k + 1) * chans, lane : lane + done]
                total = piece if total is None else total + piece
            fresh.append(ca * taken(state_ref, b + 3, 3, 0, done) + cb * total)
        for b in range(2):
            state_ref[b, :, :done] = fresh[b]

    for y in range(plan.rows):
        lane = y // 2 * stride
        out_ref[pl.ds(y, chans, stride=plan.rows), :] = state_ref[y % 2, :, lane : lane + half]


def ring(axis, step):
    count = lax.axis_size(axis)
    return [(i, i + step) for i in range(count) if 0 <= i + step < count]


def shards(latents, in_weight, mid_weight, out_weight, norm_mean, norm_rstd, cond_embed, time_embed,
           time_index, coef_index, sampler_table):
    chans, rows, cols = latents.shape
    feat = mid_weight.shape[2]
    steps = time_index.shape[0]
    half = cols // 2
    plan = Plan(rows, half, steps, chans, feat)
    margin = plan.margin
    cfg = lax.axis_index("cfg")
    swap = [(0, 1), (1, 0)]

    tail = min(rows, ceil_to(margin, 8))
    other = lax.ppermute(cond_embed, "cfg", swap)
    up = lax.ppermute(latents[:, rows - tail :], "band", ring("band", 1)).reshape(chans * tail, cols)
    dn = lax.ppermute(latents[:, :tail], "band", ring("band", -1)).reshape(chans * tail, cols)
    own = latents.reshape(chans * rows, cols)

    mask = pl.pallas_call(
        lambda *refs: mask_body(plan, ("band", "sub", "cfg"), *refs),
        out_shape=jax.ShapeDtypeStruct((2 * plan.levels, plan.block), F32),
        out_specs=VMEM,
        compiler_params=SMALL,
        cost_estimate=pl.CostEstimate(flops=8_000_000_000, transcendentals=0, bytes_accessed=200_000),
        name="masks",
    )()
    wbig, win, aff = pl.pallas_call(
        lambda *refs: prep_body(plan, "cfg", *refs),
        out_shape=[
            jax.ShapeDtypeStruct((feat, plan.depth), BF),
            jax.ShapeDtypeStruct((feat, 9 * chans), BF),
            jax.ShapeDtypeStruct((2 + 4 * steps, feat, 128), F32),
        ],
        in_specs=[SMEM] + [VMEM] * 7 + [ANY],
        out_specs=[VMEM] * 3,
        scratch_shapes=[pltpu.VMEM((128, ceil_to(feat, 128)), F32)],
        compiler_params=SMALL,
        name="prep",
    )(time_index, other, cond_embed, time_embed.T, norm_mean, norm_rstd,
      mid_weight.reshape(9 * feat, feat), in_weight.reshape(9 * chans, feat), mask)

    strip = pl.pallas_call(
        lambda *refs: pack_body(plan, tail, "cfg", *refs),
        out_shape=jax.ShapeDtypeStruct((chans, ceil_to(plan.span * margin, 128)), F32),
        in_specs=[VMEM] * 3 + [ANY],
        out_specs=VMEM,
        compiler_params=SMALL,
        name="pack",
    )(up, own, dn, win)
    subs = lax.axis_size("sub")
    pairs = []
    for i in range(subs - 1):
        pairs += [(2 * i + 1, 2 * i + 2), (2 * i + 2, 2 * i + 1)]
    side = lax.ppermute(strip, ("sub", "cfg"), pairs)

    lift, mid = max(plan.lift), max(plan.mid)
    mine = pl.pallas_call(
        lambda *refs: main_body(plan, tail, "cfg", *refs),
        out_shape=jax.ShapeDtypeStruct((chans * rows, half), F32),
        in_specs=[SMEM, SMEM] + [VMEM] * 9,
        out_specs=VMEM,
        scratch_shapes=[
            pltpu.VMEM((2, chans, plan.block), F32),
            pltpu.VMEM((2, chans, plan.block), BF),
            pltpu.VMEM((2, 2, feat, lift), BF),
            pltpu.VMEM((2, 3, feat, 4 * mid), BF),
            pltpu.VMEM((plan.depth - plan.taps, 2 * mid), BF),
            pltpu.VMEM((feat, 2 * mid), BF),
            pltpu.VMEM((9 * chans, 2 * mid + 128), F32),
        ],
        compiler_params=PARAMS,
        name="denoise",
    )(coef_index, sampler_table, own, up, dn, side, wbig, win, out_weight.reshape(9 * chans, feat), aff, mask)
    theirs = lax.ppermute(mine, "cfg", swap)
    whole = jnp.where(
        cfg == 0, jnp.concatenate([mine, theirs], axis=1), jnp.concatenate([theirs, mine], axis=1)
    )
    return whole.reshape(chans, rows, cols)


def solution(mesh):
    return jax.shard_map(
        shards,
        mesh=mesh,
        in_specs=(P("groups", "band", "sub"), P(), P(), P(), P(), P(), P("cfg", "groups"), P(), P(), P(), P()),
        out_specs=P("groups", "band", "sub"),
        check_vma=False,
    )
```

```python
import jax
import jax.numpy as jnp
from jax import lax
from jax.experimental import pallas as pl
from jax.experimental.pallas import tpu as pltpu
from jax.sharding import PartitionSpec as P

TILE = 256
BF = jnp.bfloat16
F32 = jnp.float32
ANY = pl.BlockSpec(memory_space=pl.ANY)
VMEM = pl.BlockSpec(memory_space=pltpu.VMEM)
SMEM = pl.BlockSpec(memory_space=pltpu.SMEM)
PARAMS = pltpu.CompilerParams(vmem_limit_bytes=40 * 1024 * 1024)
SMALL = pltpu.CompilerParams(vmem_limit_bytes=8 * 1024 * 1024)


def ceil_to(value, unit):
    return -(-value // unit) * unit


class Plan:
    def __init__(self, rows, half, steps, chans, feat):
        self.rows, self.half, self.steps = rows, half, steps
        self.chans, self.feat = chans, feat
        self.margin = 3 * steps
        self.span = rows + 2 * self.margin
        self.stride = half + 2 * self.margin
        self.src_rows = [self.span - 6 * s for s in range(steps)]
        self.lift = [ceil_to((r - 2) // 2 * self.stride, TILE) for r in self.src_rows]
        self.mid = [ceil_to((r - 4) // 2 * self.stride, 128) for r in self.src_rows]
        self.lift = [
            max(a, ceil_to(b + self.stride + 2, TILE)) for a, b in zip(self.lift, self.mid)
        ]
        self.block = ceil_to(max(self.lift) + 3 * self.stride + 4, 128)
        self.taps = 9 * feat
        self.depth = ceil_to(9 * (feat + chans), 128)
        self.levels = 3 * steps


def act(pre, scale, shift):
    scale = jnp.concatenate([scale] * (pre.shape[1] // 128), axis=1)
    shift = jnp.concatenate([shift] * (pre.shape[1] // 128), axis=1)
    u = pre * scale + shift
    return u + u * jnp.tanh(u)


def mask_body(plan, names, mask_ref):
    stride = plan.stride
    band, sub, cfg = names
    flat = lax.broadcasted_iota(jnp.int32, (8, plan.block), 1)
    ys = jnp.floor((flat.astype(F32) + 0.5) * (1.0 / stride)).astype(jnp.int32)
    xs = flat - ys * stride
    top = lax.axis_index(band) * plan.rows
    left = (lax.axis_index(sub) * 2 + lax.axis_index(cfg)) * plan.half
    height = plan.rows * lax.axis_size(band)
    breadth = 2 * plan.half * lax.axis_size(sub)
    for level in range(plan.levels):
        edge = plan.margin - 1 - level
        gx = xs + (left - edge)
        inx = (gx >= 0) & (gx < breadth)
        for b in range(2):
            gy = 2 * ys + (top - edge + b)
            keep = inx & (gy >= 0) & (gy < height)
            line = 2 * level + b
            mask_ref[line : line + 1, :] = jnp.where(keep, 1.0, 0.0)[0:1, :]


def prep_body(plan, mid_ref, in_ref, after_ref, wbig_ref, win_ref):
    del after_ref
    feat, chans = plan.feat, plan.chans
    for k in range(9):
        wbig_ref[:, k * feat : (k + 1) * feat] = mid_ref[k * feat : (k + 1) * feat, :]
    turned = jnp.transpose(in_ref[...].astype(F32)).astype(BF)
    win_ref[...] = turned
    wbig_ref[:, plan.taps : plan.taps + 9 * chans] = turned
    rest = plan.depth - 9 * (feat + chans)
    if rest:
        wbig_ref[:, plan.depth - rest :] = jnp.zeros((feat, rest), BF)


def aff_body(plan, cfg, time_ref, other_ref, own_ref, table_ref, mean_ref, rstd_ref, after_ref, aff_ref, rows_ref):
    del after_ref
    feat, steps = plan.feat, plan.steps
    depth = table_ref.shape[1]
    last = depth // 128 * 128
    plain = lax.axis_index(cfg) == 0
    rows_ref[...] = jnp.zeros(rows_ref.shape, F32)
    rows_ref[0:2, :feat] = mean_ref[...]
    rows_ref[2:4, :feat] = 0.5 * rstd_ref[...]
    rows_ref[4:5, :feat] = jnp.where(plain, own_ref[...], other_ref[...])
    rows_ref[5:6, :feat] = jnp.where(plain, other_ref[...], own_ref[...])
    turned = jnp.transpose(rows_ref[...])[:feat, :]
    wide = [jnp.broadcast_to(turned[:, i : i + 1], (feat, 128)) for i in range(6)]
    aff_ref[0] = wide[2]
    aff_ref[1] = wide[3]
    lanes = lax.broadcasted_iota(jnp.int32, (feat, 128), 1)
    for s in range(steps):
        start = pl.multiple_of(jnp.minimum(time_ref[s] // 128, last // 128 - 1) * 128, 128)
        block = table_ref[:, pl.ds(start, 128)]
        if last < depth:
            end = jnp.concatenate([table_ref[:, last:], jnp.zeros((feat, last + 128 - depth), F32)], axis=1)
            block = jnp.where(time_ref[s] < last, block, end)
        time = jnp.sum(jnp.where(lanes == time_ref[s] % 128, block, 0.0), axis=1, keepdims=True)
        time = jnp.broadcast_to(time, (feat, 128))
        for k in range(2):
            for q in range(2):
                aff_ref[2 + 4 * s + 2 * k + q] = (time + wide[4 + q] - wide[k]) * wide[2 + k]


def field_row(plan, y, up_ref, own_ref, dn_ref, tail):
    if y < plan.margin:
        return up_ref[pl.ds(tail - plan.margin + y, plan.chans, stride=tail), :]
    if y < plan.margin + plan.rows:
        return own_ref[pl.ds(y - plan.margin, plan.chans, stride=plan.rows), :]
    return dn_ref[pl.ds(y - plan.margin - plan.rows, plan.chans, stride=tail), :]


def pack_body(plan, tail, cfg, up_ref, own_ref, dn_ref, after_ref, out_ref):
    del after_ref
    right = lax.axis_index(cfg) == 1
    width, margin = own_ref.shape[1], plan.margin
    for y in range(plan.span):
        row = field_row(plan, y, up_ref, own_ref, dn_ref, tail)
        out_ref[:, y * margin : (y + 1) * margin] = jnp.where(right, row[:, width - margin :], row[:, :margin])


def main_body(plan, tail, cfg, index_ref, table_ref, own_ref, up_ref, dn_ref, side_ref, wbig_ref, win_ref, wout_ref,
              aff_ref, mask_ref, out_ref, state_ref, src_ref, lift_ref, taps_ref, ext_ref, low_ref, z_ref):
    stride, chans, feat, steps = plan.stride, plan.chans, plan.feat, plan.steps
    margin, half = plan.margin, plan.half
    first = lax.axis_index(cfg) == 0
    width = own_ref.shape[1]

    for y in range(plan.span):
        row = field_row(plan, y, up_ref, own_ref, dn_ref, tail)
        side = side_ref[:, y * margin : (y + 1) * margin]
        low = jnp.concatenate([side, row[:, : half + margin]], axis=1)
        high = jnp.concatenate([row[:, width - half - margin :], side], axis=1)
        lane = y // 2 * stride
        state_ref[y % 2, :, lane : lane + stride] = jnp.where(first, low, high)
    ext_ref[9 * chans :, :] = jnp.zeros((ext_ref.shape[0] - 9 * chans, ext_ref.shape[1]), BF)

    def taken(ref, row, col, start, count):
        lane = row // 2 * stride + col + start
        return ref[row % 2, :, lane : lane + count]

    for s in range(steps):
        n_src = plan.src_rows[s]
        lift, mid = plan.lift[s], plan.mid[s]
        filled = n_src // 2 * stride
        for b in range(2):
            value = state_ref[b, :, :filled]
            if s:
                line = 2 * (3 * s - 1) + b
                value = value * mask_ref[line : line + 1, :filled]
            src_ref[b, :, :filled] = value.astype(BF)
        col = 2 + 4 * s
        for b in range(2):
            for k in range(9):
                i, j = k // 3, k % 3
                ext_ref[k * chans : (k + 1) * chans, b * mid : (b + 1) * mid] = taken(
                    src_ref, b + 1 + i, 1 + j, 0, mid
                )
        for b in range(2):
            line = 6 * s + b
            for base in range(0, lift, TILE):
                window = jnp.concatenate(
                    [taken(src_ref, b + k // 3, k % 3, base, TILE) for k in range(9)], axis=0
                )
                pre = jnp.dot(win_ref[...], window, preferred_element_type=F32)
                keep = mask_ref[line : line + 1, base : base + TILE]
                for q in range(2):
                    val = act(pre, aff_ref[0], aff_ref[col + q])
                    lift_ref[q, b, :, base : base + TILE] = (val * keep).astype(BF)
        pick = index_ref[s]
        ca, cb, cg = table_ref[0, pick], table_ref[1, pick], table_ref[2, pick]
        for q in range(2):
            for bb in range(4):
                for j in range(3):
                    if bb > 1 or j:
                        taps_ref[q, j, :, bb * mid : (bb + 1) * mid] = taken(lift_ref.at[q], bb, j, 0, mid)

        def tap(q, k, base):
            i, j = k // 3, k % 3
            if j:
                return taps_ref[q, j, :, i * mid + base : i * mid + base + TILE]
            parts = []
            for lane in range(i * mid + base, i * mid + base + TILE, 128):
                bb, rest = lane // mid, lane % mid
                parts.append(lift_ref[q, bb, :, rest : rest + 128] if bb < 2 else taps_ref[q, 0, :, lane : lane + 128])
            return jnp.concatenate(parts, axis=1)

        for base in range(0, 2 * mid, TILE):
            vals = []
            for q in range(2):
                window = [tap(q, k, base) for k in range(9)] + [ext_ref[:, base : base + TILE]]
                pre = jnp.dot(wbig_ref[...], jnp.concatenate(window, axis=0), preferred_element_type=F32)
                vals.append(act(pre, aff_ref[1], aff_ref[col + 2 + q]))
            val = vals[0] + cg * (vals[1] - vals[0])
            for part in range(0, TILE, 128):
                b, lane = (base + part) // mid, (base + part) % mid
                line = 6 * s + 2 + b
                keep = mask_ref[line : line + 1, lane : lane + 128]
                low_ref[:, base + part : base + part + 128] = (val[:, part : part + 128] * keep).astype(BF)
        z_ref[:, : 2 * mid] = jnp.dot(wout_ref[...], low_ref[:, : 2 * mid], preferred_element_type=F32)
        done = (n_src - 6) // 2 * stride
        fresh = []
        for b in range(2):
            total = None
            for k in range(9):
                row = b + k // 3
                lane = row % 2 * mid + row // 2 * stride + k % 3
                piece = z_ref[k * chans : (k + 1) * chans, lane : lane + done]
                total = piece if total is None else total + piece
            fresh.append(ca * taken(state_ref, b + 3, 3, 0, done) + cb * total)
        for b in range(2):
            state_ref[b, :, :done] = fresh[b]

    for y in range(plan.rows):
        lane = y // 2 * stride
        out_ref[pl.ds(y, chans, stride=plan.rows), :] = state_ref[y % 2, :, lane : lane + half]


def ring(axis, step):
    count = lax.axis_size(axis)
    return [(i, i + step) for i in range(count) if 0 <= i + step < count]


def shards(latents, in_weight, mid_weight, out_weight, norm_mean, norm_rstd, cond_embed, time_embed,
           time_index, coef_index, sampler_table):
    chans, rows, cols = latents.shape
    feat = mid_weight.shape[2]
    steps = time_index.shape[0]
    half = cols // 2
    plan = Plan(rows, half, steps, chans, feat)
    margin = plan.margin
    cfg = lax.axis_index("cfg")
    swap = [(0, 1), (1, 0)]

    tail = min(rows, ceil_to(margin, 8))
    other = lax.ppermute(cond_embed, "cfg", swap)
    up = lax.ppermute(latents[:, rows - tail :], "band", ring("band", 1)).reshape(chans * tail, cols)
    dn = lax.ppermute(latents[:, :tail], "band", ring("band", -1)).reshape(chans * tail, cols)
    own = latents.reshape(chans * rows, cols)

    mask = pl.pallas_call(
        lambda *refs: mask_body(plan, ("band", "sub", "cfg"), *refs),
        out_shape=jax.ShapeDtypeStruct((2 * plan.levels, plan.block), F32),
        out_specs=VMEM,
        compiler_params=SMALL,
        cost_estimate=pl.CostEstimate(flops=8_000_000_000, transcendentals=0, bytes_accessed=200_000),
        name="masks",
    )()
    wbig, win = pl.pallas_call(
        lambda *refs: prep_body(plan, *refs),
        out_shape=[
            jax.ShapeDtypeStruct((feat, plan.depth), BF),
            jax.ShapeDtypeStruct((feat, 9 * chans), BF),
        ],
        in_specs=[VMEM, VMEM, ANY],
        out_specs=[VMEM] * 2,
        compiler_params=SMALL,
        name="prep",
    )(mid_weight.reshape(9 * feat, feat), in_weight.reshape(9 * chans, feat), mask)

    strip = pl.pallas_call(
        lambda *refs: pack_body(plan, tail, "cfg", *refs),
        out_shape=jax.ShapeDtypeStruct((chans, ceil_to(plan.span * margin, 128)), F32),
        in_specs=[VMEM] * 3 + [ANY],
        out_specs=VMEM,
        compiler_params=SMALL,
        name="pack",
    )(up, own, dn, win)
    subs = lax.axis_size("sub")
    pairs = []
    for i in range(subs - 1):
        pairs += [(2 * i + 1, 2 * i + 2), (2 * i + 2, 2 * i + 1)]
    side = lax.ppermute(strip, ("sub", "cfg"), pairs)

    aff = pl.pallas_call(
        lambda *refs: aff_body(plan, "cfg", *refs),
        out_shape=jax.ShapeDtypeStruct((2 + 4 * steps, feat, 128), F32),
        in_specs=[SMEM] + [VMEM] * 5 + [ANY],
        out_specs=VMEM,
        scratch_shapes=[pltpu.VMEM((128, ceil_to(feat, 128)), F32)],
        compiler_params=SMALL,
        name="affine",
    )(time_index, other, cond_embed, time_embed.T, norm_mean, norm_rstd, strip)

    lift, mid = max(plan.lift), max(plan.mid)
    mine = pl.pallas_call(
        lambda *refs: main_body(plan, tail, "cfg", *refs),
        out_shape=jax.ShapeDtypeStruct((chans * rows, half), F32),
        in_specs=[SMEM, SMEM] + [VMEM] * 9,
        out_specs=VMEM,
        scratch_shapes=[
            pltpu.VMEM((2, chans, plan.block), F32),
            pltpu.VMEM((2, chans, plan.block), BF),
            pltpu.VMEM((2, 2, feat, lift), BF),
            pltpu.VMEM((2, 3, feat, 4 * mid), BF),
            pltpu.VMEM((plan.depth - plan.taps, 2 * mid), BF),
            pltpu.VMEM((feat, 2 * mid), BF),
            pltpu.VMEM((9 * chans, 2 * mid + 128), F32),
        ],
        compiler_params=PARAMS,
        name="denoise",
    )(coef_index, sampler_table, own, up, dn, side, wbig, win, out_weight.reshape(9 * chans, feat), aff, mask)
    theirs = lax.ppermute(mine, "cfg", swap)
    whole = jnp.where(
        cfg == 0, jnp.concatenate([mine, theirs], axis=1), jnp.concatenate([theirs, mine], axis=1)
    )
    return whole.reshape(chans, rows, cols)


def solution(mesh):
    return jax.shard_map(
        shards,
        mesh=mesh,
        in_specs=(P("groups", "band", "sub"), P(), P(), P(), P(), P(), P("cfg", "groups"), P(), P(), P(), P()),
        out_specs=P("groups", "band", "sub"),
        check_vma=False,
    )
```

```python
import jax
import jax.numpy as jnp
from jax import lax
from jax.experimental import pallas as pl
from jax.experimental.pallas import tpu as pltpu
from jax.sharding import PartitionSpec as P

TILE = 256
BF = jnp.bfloat16
F32 = jnp.float32
ANY = pl.BlockSpec(memory_space=pl.ANY)
VMEM = pl.BlockSpec(memory_space=pltpu.VMEM)
SMEM = pl.BlockSpec(memory_space=pltpu.SMEM)
PARAMS = pltpu.CompilerParams(vmem_limit_bytes=40 * 1024 * 1024)
SMALL = pltpu.CompilerParams(vmem_limit_bytes=8 * 1024 * 1024)


def ceil_to(value, unit):
    return -(-value // unit) * unit


class Plan:
    def __init__(self, rows, half, steps, chans, feat):
        self.rows, self.half, self.steps = rows, half, steps
        self.chans, self.feat = chans, feat
        self.margin = 3 * steps
        self.span = rows + 2 * self.margin
        self.stride = half + 2 * self.margin
        self.src_rows = [self.span - 6 * s for s in range(steps)]
        self.lift = [ceil_to((r - 2) // 2 * self.stride, TILE) for r in self.src_rows]
        self.mid = [ceil_to((r - 4) // 2 * self.stride, 128) for r in self.src_rows]
        self.lift = [
            max(a, ceil_to(b + self.stride + 2, TILE)) for a, b in zip(self.lift, self.mid)
        ]
        self.block = ceil_to(max(self.lift) + 3 * self.stride + 4, 128)
        self.taps = 9 * feat
        self.depth = ceil_to(9 * (feat + chans), 128)
        self.levels = 3 * steps


def act(pre, scale, shift):
    scale = jnp.concatenate([scale] * (pre.shape[1] // 128), axis=1)
    shift = jnp.concatenate([shift] * (pre.shape[1] // 128), axis=1)
    u = pre * scale + shift
    return u + u * jnp.tanh(u)


def mask_body(plan, names, mask_ref):
    stride = plan.stride
    band, sub, cfg = names
    flat = lax.broadcasted_iota(jnp.int32, (8, plan.block), 1)
    ys = jnp.floor((flat.astype(F32) + 0.5) * (1.0 / stride)).astype(jnp.int32)
    xs = flat - ys * stride
    top = lax.axis_index(band) * plan.rows
    left = (lax.axis_index(sub) * 2 + lax.axis_index(cfg)) * plan.half
    height = plan.rows * lax.axis_size(band)
    breadth = 2 * plan.half * lax.axis_size(sub)
    for level in range(plan.levels):
        edge = plan.margin - 1 - level
        gx = xs + (left - edge)
        inx = (gx >= 0) & (gx < breadth)
        for b in range(2):
            gy = 2 * ys + (top - edge + b)
            keep = inx & (gy >= 0) & (gy < height)
            line = 2 * level + b
            mask_ref[line : line + 1, :] = jnp.where(keep, 1.0, 0.0)[0:1, :]


def prep_body(plan, mid_ref, in_ref, after_ref, wbig_ref, win_ref):
    del after_ref
    feat, chans = plan.feat, plan.chans
    for k in range(9):
        wbig_ref[:, k * feat : (k + 1) * feat] = mid_ref[k * feat : (k + 1) * feat, :]
    turned = jnp.transpose(in_ref[...].astype(F32)).astype(BF)
    win_ref[...] = turned
    wbig_ref[:, plan.taps : plan.taps + 9 * chans] = turned
    rest = plan.depth - 9 * (feat + chans)
    if rest:
        wbig_ref[:, plan.depth - rest :] = jnp.zeros((feat, rest), BF)


def aff_body(plan, cfg, time_ref, other_ref, own_ref, table_ref, mean_ref, rstd_ref, after_ref, aff_ref, rows_ref):
    del after_ref
    feat, steps = plan.feat, plan.steps
    depth = table_ref.shape[1]
    last = depth // 128 * 128
    plain = lax.axis_index(cfg) == 0
    rows_ref[...] = jnp.zeros(rows_ref.shape, F32)
    rows_ref[0:2, :feat] = mean_ref[...]
    rows_ref[2:4, :feat] = 0.5 * rstd_ref[...]
    rows_ref[4:5, :feat] = jnp.where(plain, own_ref[...], other_ref[...])
    rows_ref[5:6, :feat] = jnp.where(plain, other_ref[...], own_ref[...])
    turned = jnp.transpose(rows_ref[...])[:feat, :]
    wide = [jnp.broadcast_to(turned[:, i : i + 1], (feat, 128)) for i in range(6)]
    aff_ref[0] = wide[2]
    aff_ref[1] = wide[3]
    lanes = lax.broadcasted_iota(jnp.int32, (feat, 128), 1)
    for s in range(steps):
        start = pl.multiple_of(jnp.minimum(time_ref[s] // 128, last // 128 - 1) * 128, 128)
        block = table_ref[:, pl.ds(start, 128)]
        if last < depth:
            end = jnp.concatenate([table_ref[:, last:], jnp.zeros((feat, last + 128 - depth), F32)], axis=1)
            block = jnp.where(time_ref[s] < last, block, end)
        time = jnp.sum(jnp.where(lanes == time_ref[s] % 128, block, 0.0), axis=1, keepdims=True)
        time = jnp.broadcast_to(time, (feat, 128))
        for k in range(2):
            for q in range(2):
                aff_ref[2 + 4 * s + 2 * k + q] = (time + wide[4 + q] - wide[k]) * wide[2 + k]


def field_row(plan, y, up_ref, own_ref, dn_ref, tail):
    if y < plan.margin:
        return up_ref[pl.ds(tail - plan.margin + y, plan.chans, stride=tail), :]
    if y < plan.margin + plan.rows:
        return own_ref[pl.ds(y - plan.margin, plan.chans, stride=plan.rows), :]
    return dn_ref[pl.ds(y - plan.margin - plan.rows, plan.chans, stride=tail), :]


def pack_body(plan, tail, cfg, up_ref, own_ref, dn_ref, after_ref, cond_ref, out_ref):
    del after_ref, cond_ref
    right = lax.axis_index(cfg) == 1
    width, margin = own_ref.shape[1], plan.margin
    for y in range(plan.span):
        row = field_row(plan, y, up_ref, own_ref, dn_ref, tail)
        out_ref[:, y * margin : (y + 1) * margin] = jnp.where(right, row[:, width - margin :], row[:, :margin])


def main_body(plan, tail, cfg, index_ref, table_ref, own_ref, up_ref, dn_ref, side_ref, wbig_ref, win_ref, wout_ref,
              aff_ref, mask_ref, out_ref, state_ref, src_ref, lift_ref, taps_ref, ext_ref, low_ref, z_ref):
    stride, chans, feat, steps = plan.stride, plan.chans, plan.feat, plan.steps
    margin, half = plan.margin, plan.half
    first = lax.axis_index(cfg) == 0
    width = own_ref.shape[1]

    for y in range(plan.span):
        row = field_row(plan, y, up_ref, own_ref, dn_ref, tail)
        side = side_ref[:, y * margin : (y + 1) * margin]
        low = jnp.concatenate([side, row[:, : half + margin]], axis=1)
        high = jnp.concatenate([row[:, width - half - margin :], side], axis=1)
        lane = y // 2 * stride
        state_ref[y % 2, :, lane : lane + stride] = jnp.where(first, low, high)
    ext_ref[9 * chans :, :] = jnp.zeros((ext_ref.shape[0] - 9 * chans, ext_ref.shape[1]), BF)

    def taken(ref, row, col, start, count):
        lane = row // 2 * stride + col + start
        return ref[row % 2, :, lane : lane + count]

    for s in range(steps):
        n_src = plan.src_rows[s]
        lift, mid = plan.lift[s], plan.mid[s]
        filled = n_src // 2 * stride
        for b in range(2):
            value = state_ref[b, :, :filled]
            if s:
                line = 2 * (3 * s - 1) + b
                value = value * mask_ref[line : line + 1, :filled]
            src_ref[b, :, :filled] = value.astype(BF)
        col = 2 + 4 * s
        for b in range(2):
            for k in range(9):
                i, j = k // 3, k % 3
                ext_ref[k * chans : (k + 1) * chans, b * mid : (b + 1) * mid] = taken(
                    src_ref, b + 1 + i, 1 + j, 0, mid
                )
        for b in range(2):
            line = 6 * s + b
            for base in range(0, lift, TILE):
                window = jnp.concatenate(
                    [taken(src_ref, b + k // 3, k % 3, base, TILE) for k in range(9)], axis=0
                )
                pre = jnp.dot(win_ref[...], window, preferred_element_type=F32)
                keep = mask_ref[line : line + 1, base : base + TILE]
                for q in range(2):
                    val = act(pre, aff_ref[0], aff_ref[col + q])
                    lift_ref[q, b, :, base : base + TILE] = (val * keep).astype(BF)
        pick = index_ref[s]
        ca, cb, cg = table_ref[0, pick], table_ref[1, pick], table_ref[2, pick]
        for q in range(2):
            for bb in range(4):
                for j in range(3):
                    if bb > 1 or j:
                        taps_ref[q, j, :, bb * mid : (bb + 1) * mid] = taken(lift_ref.at[q], bb, j, 0, mid)

        def tap(q, k, base):
            i, j = k // 3, k % 3
            if j:
                return taps_ref[q, j, :, i * mid + base : i * mid + base + TILE]
            parts = []
            for lane in range(i * mid + base, i * mid + base + TILE, 128):
                bb, rest = lane // mid, lane % mid
                parts.append(lift_ref[q, bb, :, rest : rest + 128] if bb < 2 else taps_ref[q, 0, :, lane : lane + 128])
            return jnp.concatenate(parts, axis=1)

        for base in range(0, 2 * mid, TILE):
            vals = []
            for q in range(2):
                window = [tap(q, k, base) for k in range(9)] + [ext_ref[:, base : base + TILE]]
                pre = jnp.dot(wbig_ref[...], jnp.concatenate(window, axis=0), preferred_element_type=F32)
                vals.append(act(pre, aff_ref[1], aff_ref[col + 2 + q]))
            val = vals[0] + cg * (vals[1] - vals[0])
            for part in range(0, TILE, 128):
                b, lane = (base + part) // mid, (base + part) % mid
                line = 6 * s + 2 + b
                keep = mask_ref[line : line + 1, lane : lane + 128]
                low_ref[:, base + part : base + part + 128] = (val[:, part : part + 128] * keep).astype(BF)
        z_ref[:, : 2 * mid] = jnp.dot(wout_ref[...], low_ref[:, : 2 * mid], preferred_element_type=F32)
        done = (n_src - 6) // 2 * stride
        fresh = []
        for b in range(2):
            total = None
            for k in range(9):
                row = b + k // 3
                lane = row % 2 * mid + row // 2 * stride + k % 3
                piece = z_ref[k * chans : (k + 1) * chans, lane : lane + done]
                total = piece if total is None else total + piece
            fresh.append(ca * taken(state_ref, b + 3, 3, 0, done) + cb * total)
        for b in range(2):
            state_ref[b, :, :done] = fresh[b]

    for y in range(plan.rows):
        lane = y // 2 * stride
        out_ref[pl.ds(y, chans, stride=plan.rows), :] = state_ref[y % 2, :, lane : lane + half]


def ring(axis, step):
    count = lax.axis_size(axis)
    return [(i, i + step) for i in range(count) if 0 <= i + step < count]


def shards(latents, in_weight, mid_weight, out_weight, norm_mean, norm_rstd, cond_embed, time_embed,
           time_index, coef_index, sampler_table):
    chans, rows, cols = latents.shape
    feat = mid_weight.shape[2]
    steps = time_index.shape[0]
    half = cols // 2
    plan = Plan(rows, half, steps, chans, feat)
    margin = plan.margin
    cfg = lax.axis_index("cfg")
    swap = [(0, 1), (1, 0)]

    tail = min(rows, ceil_to(margin, 8))
    other = lax.ppermute(cond_embed, "cfg", swap)
    up = lax.ppermute(latents[:, rows - tail :], "band", ring("band", 1)).reshape(chans * tail, cols)
    dn = lax.ppermute(latents[:, :tail], "band", ring("band", -1)).reshape(chans * tail, cols)
    own = latents.reshape(chans * rows, cols)

    mask = pl.pallas_call(
        lambda *refs: mask_body(plan, ("band", "sub", "cfg"), *refs),
        out_shape=jax.ShapeDtypeStruct((2 * plan.levels, plan.block), F32),
        out_specs=VMEM,
        compiler_params=SMALL,
        cost_estimate=pl.CostEstimate(flops=8_000_000_000, transcendentals=0, bytes_accessed=200_000),
        name="masks",
    )()
    wbig, win = pl.pallas_call(
        lambda *refs: prep_body(plan, *refs),
        out_shape=[
            jax.ShapeDtypeStruct((feat, plan.depth), BF),
            jax.ShapeDtypeStruct((feat, 9 * chans), BF),
        ],
        in_specs=[VMEM, VMEM, ANY],
        out_specs=[VMEM] * 2,
        compiler_params=SMALL,
        name="prep",
    )(mid_weight.reshape(9 * feat, feat), in_weight.reshape(9 * chans, feat), mask)

    strip = pl.pallas_call(
        lambda *refs: pack_body(plan, tail, "cfg", *refs),
        out_shape=jax.ShapeDtypeStruct((chans, ceil_to(plan.span * margin, 128)), F32),
        in_specs=[VMEM] * 3 + [ANY, ANY],
        out_specs=VMEM,
        compiler_params=SMALL,
        name="pack",
    )(up, own, dn, win, other)
    subs = lax.axis_size("sub")
    pairs = []
    for i in range(subs - 1):
        pairs += [(2 * i + 1, 2 * i + 2), (2 * i + 2, 2 * i + 1)]
    side = lax.ppermute(strip, ("sub", "cfg"), pairs)

    aff = pl.pallas_call(
        lambda *refs: aff_body(plan, "cfg", *refs),
        out_shape=jax.ShapeDtypeStruct((2 + 4 * steps, feat, 128), F32),
        in_specs=[SMEM] + [VMEM] * 5 + [ANY],
        out_specs=VMEM,
        scratch_shapes=[pltpu.VMEM((128, ceil_to(feat, 128)), F32)],
        compiler_params=SMALL,
        name="affine",
    )(time_index, other, cond_embed, time_embed.T, norm_mean, norm_rstd, strip)

    lift, mid = max(plan.lift), max(plan.mid)
    mine = pl.pallas_call(
        lambda *refs: main_body(plan, tail, "cfg", *refs),
        out_shape=jax.ShapeDtypeStruct((chans * rows, half), F32),
        in_specs=[SMEM, SMEM] + [VMEM] * 9,
        out_specs=VMEM,
        scratch_shapes=[
            pltpu.VMEM((2, chans, plan.block), F32),
            pltpu.VMEM((2, chans, plan.block), BF),
            pltpu.VMEM((2, 2, feat, lift), BF),
            pltpu.VMEM((2, 3, feat, 4 * mid), BF),
            pltpu.VMEM((plan.depth - plan.taps, 2 * mid), BF),
            pltpu.VMEM((feat, 2 * mid), BF),
            pltpu.VMEM((9 * chans, 2 * mid + 128), F32),
        ],
        compiler_params=PARAMS,
        name="denoise",
    )(coef_index, sampler_table, own, up, dn, side, wbig, win, out_weight.reshape(9 * chans, feat), aff, mask)
    theirs = lax.ppermute(mine, "cfg", swap)
    whole = jnp.where(
        cfg == 0, jnp.concatenate([mine, theirs], axis=1), jnp.concatenate([theirs, mine], axis=1)
    )
    return whole.reshape(chans, rows, cols)


def solution(mesh):
    return jax.shard_map(
        shards,
        mesh=mesh,
        in_specs=(P("groups", "band", "sub"), P(), P(), P(), P(), P(), P("cfg", "groups"), P(), P(), P(), P()),
        out_specs=P("groups", "band", "sub"),
        check_vma=False,
    )
```

```python
import jax
import jax.numpy as jnp
from jax import lax
from jax.experimental import pallas as pl
from jax.experimental.pallas import tpu as pltpu
from jax.sharding import PartitionSpec as P

TILE = 256
BF = jnp.bfloat16
F32 = jnp.float32
ANY = pl.BlockSpec(memory_space=pl.ANY)
VMEM = pl.BlockSpec(memory_space=pltpu.VMEM)
SMEM = pl.BlockSpec(memory_space=pltpu.SMEM)
PARAMS = pltpu.CompilerParams(vmem_limit_bytes=40 * 1024 * 1024)
SMALL = pltpu.CompilerParams(vmem_limit_bytes=8 * 1024 * 1024)


def ceil_to(value, unit):
    return -(-value // unit) * unit


class Plan:
    def __init__(self, rows, half, steps, chans, feat):
        self.rows, self.half, self.steps = rows, half, steps
        self.chans, self.feat = chans, feat
        self.margin = 3 * steps
        self.span = rows + 2 * self.margin
        self.stride = half + 2 * self.margin
        self.src_rows = [self.span - 6 * s for s in range(steps)]
        self.lift = [ceil_to((r - 2) // 2 * self.stride, TILE) for r in self.src_rows]
        self.mid = [ceil_to((r - 4) // 2 * self.stride, 128) for r in self.src_rows]
        self.lift = [
            max(a, ceil_to(b + self.stride + 2, TILE)) for a, b in zip(self.lift, self.mid)
        ]
        self.block = ceil_to(max(self.lift) + 3 * self.stride + 4, 128)
        self.taps = 9 * feat
        self.depth = ceil_to(9 * (feat + chans), 128)
        self.levels = 3 * steps


def act(pre, scale, shift):
    scale = jnp.concatenate([scale] * (pre.shape[1] // 128), axis=1)
    shift = jnp.concatenate([shift] * (pre.shape[1] // 128), axis=1)
    u = pre * scale + shift
    return u + u * jnp.tanh(u)


def mask_body(plan, names, mask_ref):
    stride = plan.stride
    band, sub, cfg = names
    flat = lax.broadcasted_iota(jnp.int32, (8, plan.block), 1)
    ys = jnp.floor((flat.astype(F32) + 0.5) * (1.0 / stride)).astype(jnp.int32)
    xs = flat - ys * stride
    top = lax.axis_index(band) * plan.rows
    left = (lax.axis_index(sub) * 2 + lax.axis_index(cfg)) * plan.half
    height = plan.rows * lax.axis_size(band)
    breadth = 2 * plan.half * lax.axis_size(sub)
    for level in range(plan.levels):
        edge = plan.margin - 1 - level
        gx = xs + (left - edge)
        inx = (gx >= 0) & (gx < breadth)
        for b in range(2):
            gy = 2 * ys + (top - edge + b)
            keep = inx & (gy >= 0) & (gy < height)
            line = 2 * level + b
            mask_ref[line : line + 1, :] = jnp.where(keep, 1.0, 0.0)[0:1, :]


def prep_body(plan, mid_ref, in_ref, after_ref, *rest_refs):
    wbig_ref, win_ref = rest_refs[-2:]
    del after_ref
    feat, chans = plan.feat, plan.chans
    for k in range(9):
        wbig_ref[:, k * feat : (k + 1) * feat] = mid_ref[k * feat : (k + 1) * feat, :]
    turned = jnp.transpose(in_ref[...].astype(F32)).astype(BF)
    win_ref[...] = turned
    wbig_ref[:, plan.taps : plan.taps + 9 * chans] = turned
    rest = plan.depth - 9 * (feat + chans)
    if rest:
        wbig_ref[:, plan.depth - rest :] = jnp.zeros((feat, rest), BF)


def aff_body(plan, cfg, time_ref, other_ref, own_ref, table_ref, mean_ref, rstd_ref, after_ref, aff_ref, rows_ref):
    del after_ref
    feat, steps = plan.feat, plan.steps
    depth = table_ref.shape[1]
    last = depth // 128 * 128
    plain = lax.axis_index(cfg) == 0
    rows_ref[...] = jnp.zeros(rows_ref.shape, F32)
    rows_ref[0:2, :feat] = mean_ref[...]
    rows_ref[2:4, :feat] = 0.5 * rstd_ref[...]
    rows_ref[4:5, :feat] = jnp.where(plain, own_ref[...], other_ref[...])
    rows_ref[5:6, :feat] = jnp.where(plain, other_ref[...], own_ref[...])
    turned = jnp.transpose(rows_ref[...])[:feat, :]
    wide = [jnp.broadcast_to(turned[:, i : i + 1], (feat, 128)) for i in range(6)]
    aff_ref[0] = wide[2]
    aff_ref[1] = wide[3]
    lanes = lax.broadcasted_iota(jnp.int32, (feat, 128), 1)
    for s in range(steps):
        start = pl.multiple_of(jnp.minimum(time_ref[s] // 128, last // 128 - 1) * 128, 128)
        block = table_ref[:, pl.ds(start, 128)]
        if last < depth:
            end = jnp.concatenate([table_ref[:, last:], jnp.zeros((feat, last + 128 - depth), F32)], axis=1)
            block = jnp.where(time_ref[s] < last, block, end)
        time = jnp.sum(jnp.where(lanes == time_ref[s] % 128, block, 0.0), axis=1, keepdims=True)
        time = jnp.broadcast_to(time, (feat, 128))
        for k in range(2):
            for q in range(2):
                aff_ref[2 + 4 * s + 2 * k + q] = (time + wide[4 + q] - wide[k]) * wide[2 + k]


def field_row(plan, y, up_ref, own_ref, dn_ref, tail):
    if y < plan.margin:
        return up_ref[pl.ds(tail - plan.margin + y, plan.chans, stride=tail), :]
    if y < plan.margin + plan.rows:
        return own_ref[pl.ds(y - plan.margin, plan.chans, stride=plan.rows), :]
    return dn_ref[pl.ds(y - plan.margin - plan.rows, plan.chans, stride=tail), :]


def pack_body(plan, tail, cfg, up_ref, own_ref, dn_ref, after_ref, cond_ref, out_ref):
    del after_ref, cond_ref
    right = lax.axis_index(cfg) == 1
    width, margin = own_ref.shape[1], plan.margin
    for y in range(plan.span):
        row = field_row(plan, y, up_ref, own_ref, dn_ref, tail)
        out_ref[:, y * margin : (y + 1) * margin] = jnp.where(right, row[:, width - margin :], row[:, :margin])


def main_body(plan, tail, cfg, index_ref, table_ref, own_ref, up_ref, dn_ref, side_ref, wbig_ref, win_ref, wout_ref,
              aff_ref, mask_ref, out_ref, state_ref, src_ref, lift_ref, taps_ref, ext_ref, low_ref, z_ref):
    stride, chans, feat, steps = plan.stride, plan.chans, plan.feat, plan.steps
    margin, half = plan.margin, plan.half
    first = lax.axis_index(cfg) == 0
    width = own_ref.shape[1]

    for y in range(plan.span):
        row = field_row(plan, y, up_ref, own_ref, dn_ref, tail)
        side = side_ref[:, y * margin : (y + 1) * margin]
        low = jnp.concatenate([side, row[:, : half + margin]], axis=1)
        high = jnp.concatenate([row[:, width - half - margin :], side], axis=1)
        lane = y // 2 * stride
        state_ref[y % 2, :, lane : lane + stride] = jnp.where(first, low, high)
    ext_ref[9 * chans :, :] = jnp.zeros((ext_ref.shape[0] - 9 * chans, ext_ref.shape[1]), BF)

    def taken(ref, row, col, start, count):
        lane = row // 2 * stride + col + start
        return ref[row % 2, :, lane : lane + count]

    for s in range(steps):
        n_src = plan.src_rows[s]
        lift, mid = plan.lift[s], plan.mid[s]
        filled = n_src // 2 * stride
        for b in range(2):
            value = state_ref[b, :, :filled]
            if s:
                line = 2 * (3 * s - 1) + b
                value = value * mask_ref[line : line + 1, :filled]
            src_ref[b, :, :filled] = value.astype(BF)
        col = 2 + 4 * s
        for b in range(2):
            for k in range(9):
                i, j = k // 3, k % 3
                ext_ref[k * chans : (k + 1) * chans, b * mid : (b + 1) * mid] = taken(
                    src_ref, b + 1 + i, 1 + j, 0, mid
                )
        for b in range(2):
            line = 6 * s + b
            for base in range(0, lift, TILE):
                window = jnp.concatenate(
                    [taken(src_ref, b + k // 3, k % 3, base, TILE) for k in range(9)], axis=0
                )
                pre = jnp.dot(win_ref[...], window, preferred_element_type=F32)
                keep = mask_ref[line : line + 1, base : base + TILE]
                for q in range(2):
                    val = act(pre, aff_ref[0], aff_ref[col + q])
                    lift_ref[q, b, :, base : base + TILE] = (val * keep).astype(BF)
        pick = index_ref[s]
        ca, cb, cg = table_ref[0, pick], table_ref[1, pick], table_ref[2, pick]
        for q in range(2):
            for bb in range(4):
                for j in range(3):
                    if bb > 1 or j:
                        taps_ref[q, j, :, bb * mid : (bb + 1) * mid] = taken(lift_ref.at[q], bb, j, 0, mid)

        def tap(q, k, base):
            i, j = k // 3, k % 3
            if j:
                return taps_ref[q, j, :, i * mid + base : i * mid + base + TILE]
            parts = []
            for lane in range(i * mid + base, i * mid + base + TILE, 128):
                bb, rest = lane // mid, lane % mid
                parts.append(lift_ref[q, bb, :, rest : rest + 128] if bb < 2 else taps_ref[q, 0, :, lane : lane + 128])
            return jnp.concatenate(parts, axis=1)

        for base in range(0, 2 * mid, TILE):
            vals = []
            for q in range(2):
                window = [tap(q, k, base) for k in range(9)] + [ext_ref[:, base : base + TILE]]
                pre = jnp.dot(wbig_ref[...], jnp.concatenate(window, axis=0), preferred_element_type=F32)
                vals.append(act(pre, aff_ref[1], aff_ref[col + 2 + q]))
            val = vals[0] + cg * (vals[1] - vals[0])
            for part in range(0, TILE, 128):
                b, lane = (base + part) // mid, (base + part) % mid
                line = 6 * s + 2 + b
                keep = mask_ref[line : line + 1, lane : lane + 128]
                low_ref[:, base + part : base + part + 128] = (val[:, part : part + 128] * keep).astype(BF)
        z_ref[:, : 2 * mid] = jnp.dot(wout_ref[...], low_ref[:, : 2 * mid], preferred_element_type=F32)
        done = (n_src - 6) // 2 * stride
        fresh = []
        for b in range(2):
            total = None
            for k in range(9):
                row = b + k // 3
                lane = row % 2 * mid + row // 2 * stride + k % 3
                piece = z_ref[k * chans : (k + 1) * chans, lane : lane + done]
                total = piece if total is None else total + piece
            fresh.append(ca * taken(state_ref, b + 3, 3, 0, done) + cb * total)
        for b in range(2):
            state_ref[b, :, :done] = fresh[b]

    for y in range(plan.rows):
        lane = y // 2 * stride
        out_ref[pl.ds(y, chans, stride=plan.rows), :] = state_ref[y % 2, :, lane : lane + half]


def ring(axis, step):
    count = lax.axis_size(axis)
    return [(i, i + step) for i in range(count) if 0 <= i + step < count]


def shards(latents, in_weight, mid_weight, out_weight, norm_mean, norm_rstd, cond_embed, time_embed,
           time_index, coef_index, sampler_table):
    chans, rows, cols = latents.shape
    feat = mid_weight.shape[2]
    steps = time_index.shape[0]
    half = cols // 2
    plan = Plan(rows, half, steps, chans, feat)
    margin = plan.margin
    cfg = lax.axis_index("cfg")
    swap = [(0, 1), (1, 0)]

    tail = min(rows, ceil_to(margin, 8))
    other = lax.ppermute(cond_embed, "cfg", swap)
    up = lax.ppermute(latents[:, rows - tail :], "band", ring("band", 1)).reshape(chans * tail, cols)
    dn = lax.ppermute(latents[:, :tail], "band", ring("band", -1)).reshape(chans * tail, cols)
    own = latents.reshape(chans * rows, cols)

    mask = pl.pallas_call(
        lambda *refs: mask_body(plan, ("band", "sub", "cfg"), *refs),
        out_shape=jax.ShapeDtypeStruct((2 * plan.levels, plan.block), F32),
        out_specs=VMEM,
        compiler_params=SMALL,
        cost_estimate=pl.CostEstimate(flops=8_000_000_000, transcendentals=0, bytes_accessed=200_000),
        name="masks",
    )()
    wbig, win = pl.pallas_call(
        lambda *refs: prep_body(plan, *refs),
        out_shape=[
            jax.ShapeDtypeStruct((feat, plan.depth), BF),
            jax.ShapeDtypeStruct((feat, 9 * chans), BF),
        ],
        in_specs=[VMEM, VMEM, ANY] + [VMEM] * 5,
        out_specs=[VMEM] * 2,
        compiler_params=SMALL,
        name="prep",
    )(mid_weight.reshape(9 * feat, feat), in_weight.reshape(9 * chans, feat), mask,
      time_embed.T, norm_mean, norm_rstd, cond_embed, out_weight.reshape(9 * chans, feat))

    strip = pl.pallas_call(
        lambda *refs: pack_body(plan, tail, "cfg", *refs),
        out_shape=jax.ShapeDtypeStruct((chans, ceil_to(plan.span * margin, 128)), F32),
        in_specs=[VMEM] * 3 + [ANY, ANY],
        out_specs=VMEM,
        compiler_params=SMALL,
        name="pack",
    )(up, own, dn, win, other)
    subs = lax.axis_size("sub")
    pairs = []
    for i in range(subs - 1):
        pairs += [(2 * i + 1, 2 * i + 2), (2 * i + 2, 2 * i + 1)]
    side = lax.ppermute(strip, ("sub", "cfg"), pairs)

    aff = pl.pallas_call(
        lambda *refs: aff_body(plan, "cfg", *refs),
        out_shape=jax.ShapeDtypeStruct((2 + 4 * steps, feat, 128), F32),
        in_specs=[SMEM] + [VMEM] * 5 + [ANY],
        out_specs=VMEM,
        scratch_shapes=[pltpu.VMEM((128, ceil_to(feat, 128)), F32)],
        compiler_params=SMALL,
        name="affine",
    )(time_index, other, cond_embed, time_embed.T, norm_mean, norm_rstd, strip)

    lift, mid = max(plan.lift), max(plan.mid)
    mine = pl.pallas_call(
        lambda *refs: main_body(plan, tail, "cfg", *refs),
        out_shape=jax.ShapeDtypeStruct((chans * rows, half), F32),
        in_specs=[SMEM, SMEM] + [VMEM] * 9,
        out_specs=VMEM,
        scratch_shapes=[
            pltpu.VMEM((2, chans, plan.block), F32),
            pltpu.VMEM((2, chans, plan.block), BF),
            pltpu.VMEM((2, 2, feat, lift), BF),
            pltpu.VMEM((2, 3, feat, 4 * mid), BF),
            pltpu.VMEM((plan.depth - plan.taps, 2 * mid), BF),
            pltpu.VMEM((feat, 2 * mid), BF),
            pltpu.VMEM((9 * chans, 2 * mid + 128), F32),
        ],
        compiler_params=PARAMS,
        name="denoise",
    )(coef_index, sampler_table, own, up, dn, side, wbig, win, out_weight.reshape(9 * chans, feat), aff, mask)
    theirs = lax.ppermute(mine, "cfg", swap)
    whole = jnp.where(
        cfg == 0, jnp.concatenate([mine, theirs], axis=1), jnp.concatenate([theirs, mine], axis=1)
    )
    return whole.reshape(chans, rows, cols)


def solution(mesh):
    return jax.shard_map(
        shards,
        mesh=mesh,
        in_specs=(P("groups", "band", "sub"), P(), P(), P(), P(), P(), P("cfg", "groups"), P(), P(), P(), P()),
        out_specs=P("groups", "band", "sub"),
        check_vma=False,
    )
```
